32 devices in a mesh: groups: 2 (over x), ctx: 16 (over z, y, core).
Axes of the slice: x: 2, y: 2, z: 4, core: 2. Of those that a mesh axis runs over, the one named last changes fastest.
Arguments:
- raster_tokens: bfloat16 [4096, 1024], P(('groups', 'ctx')), parts along dimension 0, may hold values from -45 to 45
- hilbert_perm: int32 [4096], P(('groups', 'ctx')), parts along dimension 0, may hold values from 0 to 2047, as said below
- neighbors: int32 [32, 5], P(('groups', 'ctx')), parts along dimension 0, may hold values from 0 to 15, as said below
- neighbor_counts: int32 [32], P(('groups', 'ctx')), parts along dimension 0, may hold values from 1 to 5, as said below
- norm_gain: float32 [1024], replicated, may hold values from 0.1 to 1.9
- w_qkv: bfloat16 [1024, 3072], replicated, may hold values from -0.8125 to 0.8125
- w_out: bfloat16 [1024, 1024], replicated, may hold values from -0.5 to 0.5
- cotangent: bfloat16 [4096, 1024], P(('groups', 'ctx')), parts along dimension 0, may hold values from -6 to 6
Outputs:
- layer_out: bfloat16 [4096, 1024], P(('groups', 'ctx')), parts along dimension 0
- grad_tokens: bfloat16 [4096, 1024], P(('groups', 'ctx')), parts along dimension 0
- grad_w_out: float32 [2048, 1024], P(('groups', 'ctx')), parts along dimension 0
- grad_gain: float32 [2048], P('groups'), parts along dimension 0
The draws below stay inside these ranges and needn't reach their ends.
There are 2 independent parts, one for each index of `groups`. The reference program is written for one: setup_inputs(seed, part) draws one part's arguments, and reference() takes and returns one part's arrays. A program takes and returns all parts, laid end to end along the dimension named above; an argument that names none is the same for every part. Nothing has to cross between parts.
Inputs may be any that keep to these rules, and one draw needn't show every extreme that they name: `hilbert_perm`: A permutation. Every 128 consecutive positions of the Hilbert order take exactly 8 tokens from every 128 consecutive raster tokens. `neighbors`: row b starts with b, followed by distinct blocks other than b at a distance of at most 4; entries from slot neighbor_counts[b] on equal b. `neighbor_counts`: the block itself is counted.
All inputs are finite; a program needn't handle non-finite values.
Results may differ from the reference program's by a relative error of at most 0.02.
The reference program's roundings to bfloat16 on the way count: a program that leaves them out, or rounds other values in their place, can miss the bound.
Values may be sent and summed in bfloat16 or wider, within the bound.
No kernel may reach another device: no remote copies, remote signals or barrier semaphores. Data moves between devices by JAX's collectives and lax.ppermute only.
A program may use at most 128 MiB of HBM per device.

```python
import math
import jax
import jax.numpy as jnp
from jax import lax

D = 1024
HEADS = 16
HD = 64
BLOCK = 128
MOST = 5
REACH = 4
TOK_DEV = 128
TOKENS = 2048
BPD = 1
NBLK = 16
WIN_DEV = 4
N_CTX = 16


def perm_core(key):
    dev_count = TOKENS // TOK_DEV
    per_peer = TOK_DEV // dev_count
    key_slots, key_rows = jax.random.split(jax.random.fold_in(key, 11))
    slot_perm = jax.vmap(lambda sub_key: jax.random.permutation(sub_key, TOK_DEV))(jax.random.split(key_slots, dev_count))
    row_perm = jax.vmap(lambda sub_key: jax.random.permutation(sub_key, TOK_DEV))(jax.random.split(key_rows, dev_count))
    source_dev = slot_perm // per_peer
    rank_in = slot_perm % per_peer
    dest_dev = jnp.arange(dev_count)[:, None]
    picked = row_perm[source_dev, dest_dev * per_peer + rank_in]
    return (source_dev * TOK_DEV + picked).reshape(-1).astype(jnp.int32)


def adjacency_core(key):
    key_pick, key_count, key_force = jax.random.split(jax.random.fold_in(key, 7), 3)
    offsets = jnp.concatenate([jnp.arange(-REACH, 0), jnp.arange(1, REACH + 1)])
    blocks = jnp.arange(NBLK)[:, None]
    candidate = blocks + offsets[None, :]
    inside = (candidate >= 0) & (candidate < NBLK)
    ranking = jax.random.randint(key_pick, (NBLK, 2 * REACH), 0, 4096) * (2 * REACH) + jnp.arange(2 * REACH)[None, :]
    ranking = jnp.where(inside, ranking, -1)
    top_values, top_index = lax.top_k(ranking, MOST - 1)
    chosen = jnp.take_along_axis(candidate, top_index, axis=1)
    counts = jax.random.randint(key_count, (NBLK,), 1, MOST + 1)
    forced = jax.random.randint(key_force, (), 0, NBLK)
    counts = jnp.where(jnp.arange(NBLK) == forced, MOST, counts)
    slot_ids = jnp.arange(1, MOST)[None, :]
    chosen = jnp.where(slot_ids < counts[:, None], chosen, blocks)
    lists = jnp.concatenate([blocks, chosen], axis=1).astype(jnp.int32)
    return (lists, counts.astype(jnp.int32))


def draw_hilbert_perm(key, part):
    return perm_core(key)


def draw_neighbors(key, part):
    lists, counts = adjacency_core(key)
    return lists


def draw_neighbor_counts(key, part):
    lists, counts = adjacency_core(key)
    return counts


def draw_raster_tokens(key, part):
    key_base, key_rows, key_cols = jax.random.split(jax.random.fold_in(key, 3), 3)
    normal_part = jax.random.truncated_normal(key_base, -4.0, 4.0, (TOKENS, D), jnp.float32)
    row_scale = jnp.exp(jax.random.uniform(key_rows, (TOKENS, 1), jnp.float32, math.log(0.3), math.log(3.0)))
    col_scale = jnp.exp(jax.random.uniform(key_cols, (1, D), jnp.float32, math.log(0.3), math.log(3.0)))
    values = normal_part * row_scale * col_scale
    return values.astype(jnp.bfloat16)


def draw_w_qkv(key, part):
    key_base = jax.random.fold_in(jax.random.fold_in(key, 5), 0)
    normal_part = jax.random.truncated_normal(key_base, -4.0, 4.0, (D, 3 * D), jnp.float32) * D ** (-0.5)
    return normal_part.astype(jnp.bfloat16)


def level_of(key, extent, cuts, low, top_value):
    def one(axis_at, shards_of):
        steps = jax.random.uniform(jax.random.fold_in(jax.random.fold_in(key, 6), axis_at), (shards_of,), jnp.float32, low / len(cuts), top_value / len(cuts))
        return jnp.repeat(jnp.exp(steps), extent[axis_at] // shards_of).reshape((-1,) + (1,) * (len(extent) - axis_at - 1))

    gain = one(*cuts[0])
    for cut in cuts[1:]:
        gain = gain * one(*cut)
    return gain


def normal_values(stream_key, shape, width, limit, shards=(), held_as=jnp.bfloat16):
    values = jax.random.normal(stream_key, shape, jnp.float32) * width
    if len(shards) > 0:
        values = level_of(stream_key, shape, shards, -0.22, 0.18) * values
    return jnp.clip(values, min=-limit, max=limit).astype(held_as)


def setup_inputs(seed: int = 0, part: int = 0) -> dict:
    key_list = jax.random.split(jax.random.key(seed), 9)
    own_keys = jax.random.split(jax.random.fold_in(key_list[8], part), 9)
    return {
        "raster_tokens": draw_raster_tokens(jax.random.fold_in(jax.random.fold_in(key_list[8], part), 71), part),
        "hilbert_perm": draw_hilbert_perm(jax.random.fold_in(jax.random.fold_in(key_list[8], part), 71), part),
        "neighbors": draw_neighbors(jax.random.fold_in(jax.random.fold_in(key_list[8], part), 71), part),
        "neighbor_counts": draw_neighbor_counts(jax.random.fold_in(jax.random.fold_in(key_list[8], part), 71), part),
        "norm_gain": jnp.clip(1.0 + 0.18 * jax.random.normal(key_list[4], (D,), jnp.float32), 0.1, 1.9),
        "w_qkv": draw_w_qkv(jax.random.fold_in(key_list[8], 71), part),
        "w_out": normal_values(key_list[6], (D, D), (D // 8) ** -0.5, 0.5),
        "cotangent": normal_values(own_keys[7], (TOKENS, D), 1.0, 6.0, ((0, 16),)),
    }


EPS = 1e-06
FAR = -1e+30

def probs_of(heads_q, heads_k, counts):
    scores = jnp.einsum('sqhd,skhd->shqk', heads_q.astype(jnp.float32), heads_k.astype(jnp.float32), precision=lax.Precision.HIGHEST) * HD ** (-0.5)
    slot_of = jnp.arange(heads_k.shape[1]) // BLOCK
    usable = slot_of[None, :] < counts[:, None]
    scores = jnp.where(usable[:, None, None, :], scores, FAR)
    row_max = lax.optimization_barrier(jnp.max(scores, axis=-1, keepdims=True))
    shifted = jnp.exp(scores - row_max)
    return shifted / lax.optimization_barrier(jnp.sum(shifted, axis=-1, keepdims=True))

def reference(raster_tokens, hilbert_perm, neighbors, neighbor_counts, norm_gain, w_qkv, w_out, cotangent):
    ordered = raster_tokens[hilbert_perm]
    ordered_f = ordered.astype(jnp.float32)
    inv_rms = lax.rsqrt(lax.optimization_barrier(jnp.mean(ordered_f * ordered_f, axis=-1, keepdims=True)) + EPS)
    normed = (ordered_f * inv_rms * norm_gain).astype(jnp.bfloat16)
    projected = jnp.dot(normed, w_qkv, preferred_element_type=jnp.float32).astype(jnp.bfloat16)
    queries = projected[:, :D]
    keys_vals = projected[:, D:]
    pad_rows = WIN_DEV * TOK_DEV
    span_rows = (2 * WIN_DEV + 1) * TOK_DEV
    kv_pad = jnp.pad(keys_vals, ((pad_rows, pad_rows), (0, 0)))
    dev_ids = jnp.arange(N_CTX, dtype=jnp.int32)

    def local_view(dev_index):
        window = lax.dynamic_slice_in_dim(kv_pad, dev_index * TOK_DEV, span_rows, 0)
        blocks = window.reshape(-1, BLOCK, 2 * D)
        lists = lax.dynamic_slice_in_dim(neighbors, dev_index * BPD, BPD, 0)
        slot_index = (lists - (dev_index - WIN_DEV) * BPD).astype(jnp.int32)
        picked = blocks[slot_index].reshape(BPD, MOST * BLOCK, 2 * D)
        heads_k = picked[:, :, :D].reshape(BPD, MOST * BLOCK, HEADS, HD)
        heads_v = picked[:, :, D:].reshape(BPD, MOST * BLOCK, HEADS, HD)
        q_rows = lax.dynamic_slice_in_dim(queries, dev_index * TOK_DEV, TOK_DEV, 0)
        heads_q = q_rows.reshape(BPD, BLOCK, HEADS, HD)
        counts = lax.dynamic_slice_in_dim(neighbor_counts, dev_index * BPD, BPD, 0)
        weights_f = probs_of(heads_q, heads_k, counts)
        return (heads_q, heads_k, heads_v, slot_index, weights_f)

    def forward_pass(dev_index):
        heads_q, heads_k, heads_v, slot_index, weights_f = local_view(dev_index)
        probs_b = weights_f.astype(jnp.bfloat16)
        out_rows = jnp.einsum('shqk,skhd->sqhd', probs_b.astype(jnp.float32), heads_v.astype(jnp.float32), precision=lax.Precision.HIGHEST)
        return out_rows.reshape(TOK_DEV, D).astype(jnp.bfloat16)
    attended = lax.map(forward_pass, dev_ids).reshape(TOKENS, D)
    projected_out = jnp.dot(attended, w_out, preferred_element_type=jnp.float32)
    layer_out = (ordered_f + projected_out).astype(jnp.bfloat16)
    norm_scale = TOKENS ** (-0.5)
    grad_w_out = lax.dot_general(attended, cotangent, (((0,), (0,)), ((), ())), preferred_element_type=jnp.float32) * norm_scale
    d_attended = jnp.dot(cotangent, w_out.T, preferred_element_type=jnp.float32).astype(jnp.bfloat16)

    def backward_pass(dev_index):
        heads_q, heads_k, heads_v, slot_index, weights_f = local_view(dev_index)
        probs_b = weights_f.astype(jnp.bfloat16)
        d_rows = lax.dynamic_slice_in_dim(d_attended, dev_index * TOK_DEV, TOK_DEV, 0)
        d_heads = d_rows.reshape(BPD, BLOCK, HEADS, HD).astype(jnp.float32)
        d_probs = jnp.einsum('sqhd,skhd->shqk', d_heads, heads_v.astype(jnp.float32), precision=lax.Precision.HIGHEST)
        row_dots = lax.optimization_barrier(jnp.sum(d_probs * weights_f, axis=-1, keepdims=True))
        d_scores = (weights_f * (d_probs - row_dots) * HD ** (-0.5)).astype(jnp.bfloat16).astype(jnp.float32)
        d_query = jnp.einsum('shqk,skhd->sqhd', d_scores, heads_k.astype(jnp.float32), precision=lax.Precision.HIGHEST)
        d_query = d_query.reshape(TOK_DEV, D).astype(jnp.bfloat16)
        d_keys = jnp.einsum('shqk,sqhd->skhd', d_scores, heads_q.astype(jnp.float32), precision=lax.Precision.HIGHEST)
        d_vals = jnp.einsum('shqk,sqhd->skhd', probs_b.astype(jnp.float32), d_heads, precision=lax.Precision.HIGHEST)
        contrib = jnp.concatenate([d_keys.reshape(BPD * MOST, BLOCK, D), d_vals.reshape(BPD * MOST, BLOCK, D)], axis=-1)
        summed = jnp.zeros(((2 * WIN_DEV + 1) * BPD, BLOCK, 2 * D), jnp.float32).at[slot_index.reshape(-1)].add(contrib)
        return (d_query, summed.reshape(span_rows, 2 * D).astype(jnp.bfloat16))
    d_query_all, partials = lax.map(backward_pass, dev_ids)
    d_query_all = d_query_all.reshape(TOKENS, D)
    partials = partials.reshape(N_CTX, 2 * WIN_DEV + 1, TOK_DEV, 2 * D)
    accum = jnp.zeros((N_CTX, TOK_DEV, 2 * D), jnp.float32)
    for offset in range(2 * WIN_DEV + 1):
        layer_piece = partials[:, offset].astype(jnp.float32)
        padded = jnp.pad(layer_piece, ((WIN_DEV, WIN_DEV), (0, 0), (0, 0)))
        accum = accum + padded[2 * WIN_DEV - offset:2 * WIN_DEV - offset + N_CTX]
    d_kv = accum.reshape(TOKENS, 2 * D).astype(jnp.bfloat16)
    d_proj = jnp.concatenate([d_query_all, d_kv], axis=-1)
    d_normed = jnp.dot(d_proj, w_qkv.T, preferred_element_type=jnp.float32)
    grad_gain = lax.optimization_barrier(jnp.sum(d_normed * ordered_f * inv_rms, axis=0)) * norm_scale
    scaled = d_normed * norm_gain
    d_ordered = cotangent.astype(jnp.float32) + inv_rms * scaled - ordered_f * inv_rms ** 3 * lax.optimization_barrier(jnp.mean(scaled * ordered_f, axis=-1, keepdims=True))
    d_ordered = d_ordered.astype(jnp.bfloat16)
    grad_tokens = jnp.zeros_like(raster_tokens).at[hilbert_perm].set(d_ordered)
    return (layer_out, grad_tokens, grad_w_out, grad_gain)
```

```python
import functools

import jax
import jax.numpy as jnp
from jax import lax
from jax.experimental import pallas as pl
from jax.experimental.pallas import tpu as pltpu
from jax.sharding import PartitionSpec as P

HEADS = 16
BLOCK = 128
LANES = 128
EPS = 1e-06
FAR = -1e30
F32 = jnp.float32
BF16 = jnp.bfloat16


def iota(shape, dim):
    return lax.broadcasted_iota(jnp.int32, shape, dim)


def nn(a, b):
    return jnp.dot(a, b, preferred_element_type=F32)


def nt(a, b):
    return lax.dot_general(a, b, (((1,), (1,)), ((), ())), preferred_element_type=F32)


def tn(a, b):
    return lax.dot_general(a, b, (((0,), (0,)), ((), ())), preferred_element_type=F32)


def ranks(key_col, key_row, dim):
    if dim == 0:
        return jnp.sum((key_col < key_row).astype(F32), axis=0, keepdims=True).astype(jnp.int32)
    return jnp.sum((key_row < key_col).astype(F32), axis=1, keepdims=True).astype(jnp.int32)


def column_of(row):
    n = row.shape[1]
    wide = jnp.broadcast_to(row.astype(F32), (n, n))
    return jnp.transpose(wide)[:, :1].astype(jnp.int32)


def row_of(col):
    n = col.shape[0]
    wide = jnp.broadcast_to(col.astype(F32), (n, n))
    return jnp.transpose(wide)[:1, :].astype(jnp.int32)


def pack_kernel(n_dev, slots, per_peer, owners_ref, table_ref, perm_ref, raster_ref, msg_ref, one_ref, sorted_ref):
    rows = raster_ref.shape[1]
    for part in range(raster_ref.shape[0]):
        target = owners_ref[part] * rows + iota((rows, 1), 0)

        def hit(block, acc):
            line = perm_ref[pl.ds(block, 1), :]
            return acc + jnp.where(line == target, block, 0)

        found = lax.fori_loop(0, n_dev, hit, jnp.zeros((rows, rows), jnp.int32), unroll=4)
        home = jnp.sum(found.astype(F32), axis=1, keepdims=True).astype(jnp.int32)
        key_col = home * rows + iota((rows, 1), 0)
        key_row = row_of(key_col)
        slot_row = ranks(key_col, key_row, 0)
        slot_col = ranks(key_col, key_row, 1)
        pick = (slot_row == iota((rows, rows), 0)).astype(BF16)
        one_ref[part] = (slot_col == iota((rows, rows), 1)).astype(BF16)
        ordered = nn(pick, raster_ref[part]).astype(BF16)
        if per_peer % 8 == 0:
            sorted_ref[part] = ordered.astype(F32).reshape(n_dev, per_peer, -1)
        else:
            sorted_ref[part] = ordered
    if per_peer % 8 == 0:
        n_dest = msg_ref.shape[0]
        for part in range(raster_ref.shape[0]):

            def place(dest, carry):
                for slot in range(slots):
                    block = table_ref[dest, slot]
                    msg_ref[dest, part, slot] = sorted_ref[part, block].astype(BF16)
                return carry

            lax.fori_loop(0, n_dest, place, 0, unroll=2)


def main_kernel(
    count_ref, arrived_ref, perm_ref, gain_ref, cot_ref, wqkv_ref, wout_ref,
    layer_ref, ret_ref, gain_out_ref, att_ref, cots_ref,
    x_ref, inv_ref, nrm_ref, q_ref, kv_ref, do_ref, attf_ref, dq_ref, dkv_ref,
):
    n_rows, width = x_ref.shape
    slots = n_rows // BLOCK
    head_dim = width // HEADS
    gain = gain_ref[...]
    key_row = perm_ref[...]
    key_col = column_of(key_row)
    slot_row = ranks(key_col, key_row, 0)
    slot_col = ranks(key_col, key_row, 1)
    to_arrival = (slot_row == iota((BLOCK, BLOCK), 0)).astype(BF16)
    to_order = (slot_col == iota((BLOCK, BLOCK), 1)).astype(BF16)
    cots_ref[...] = nn(to_arrival, cot_ref[...]).astype(BF16)
    for j in range(slots):
        x = arrived_ref[:, j].astype(F32).reshape(BLOCK, width)
        x_ref[pl.ds(j * BLOCK, BLOCK), :] = x
        inv = lax.rsqrt(jnp.mean(x * x, axis=1, keepdims=True) + EPS)
        inv_ref[pl.ds(j * BLOCK, BLOCK), :] = jnp.broadcast_to(inv, (BLOCK, LANES))
        nrm_ref[pl.ds(j * BLOCK, BLOCK), :] = (x * inv * gain).astype(BF16)
    scale = head_dim ** (-0.5)
    q_ref[...] = nn(nrm_ref[pl.ds(0, BLOCK), :], wqkv_ref[:, :width]).astype(BF16)
    kv_ref[...] = nn(nrm_ref[...], wqkv_ref[:, width:]).astype(BF16)
    do_ref[...] = nt(cots_ref[...], wout_ref[...]).astype(BF16)
    count = count_ref[0]
    first = iota((BLOCK, LANES), 1) < head_dim

    def both(pair):
        zero = jnp.zeros_like(pair)
        return jnp.concatenate([jnp.where(first, pair, zero), jnp.where(first, zero, pair)], axis=0)

    def own(out):
        return jnp.concatenate([out[:head_dim, :BLOCK], out[head_dim:, BLOCK:]], axis=0)

    def pair_step(pair, carry):
        lane = pl.multiple_of(pair * LANES, LANES)
        cols = pl.ds(lane, LANES)
        vcols = pl.ds(pl.multiple_of(width + pair * LANES, LANES), LANES)
        qm = both(q_ref[:, cols])
        dom = both(do_ref[:, cols])
        k = kv_ref[:, cols]
        v = kv_ref[:, vcols]
        s = nt(k, qm) * scale
        s = jnp.concatenate(
            [jnp.where(j < count, s[j * BLOCK:(j + 1) * BLOCK], FAR) for j in range(slots)], axis=0
        )
        e = jnp.exp(s - jnp.max(s, axis=0, keepdims=True))
        p = e / jnp.sum(e, axis=0, keepdims=True)
        pb = p.astype(BF16)
        dp = nt(v, dom)
        dots = jnp.sum(dp * p, axis=0, keepdims=True)
        ds = (p * (dp - dots) * scale).astype(BF16)
        attf_ref[:, cols] = jnp.transpose(own(tn(v, pb)))
        dq_ref[:, cols] = jnp.transpose(own(tn(k, ds))).astype(BF16)
        dkv_ref[:, cols] = nn(ds, qm).astype(BF16)
        dkv_ref[:, vcols] = nn(pb, dom).astype(BF16)
        return carry

    lax.fori_loop(0, width // LANES, pair_step, 0)
    att = attf_ref[...].astype(BF16)
    att_ref[...] = att
    layer = (x_ref[pl.ds(0, BLOCK), :] + nn(att, wout_ref[...])).astype(BF16)
    layer_ref[...] = nn(to_order, layer).astype(BF16)
    gains = jnp.zeros((1, width), F32)
    for j in range(slots):
        rows = pl.ds(j * BLOCK, BLOCK)
        dn = nt(dkv_ref[rows, :], wqkv_ref[:, width:])
        if j == 0:
            dn = dn + nt(dq_ref[...], wqkv_ref[:, :width])
        x = x_ref[rows, :]
        inv = inv_ref[rows, :][:, :1]
        gains = gains + jnp.sum(dn * (x * inv), axis=0, keepdims=True)
        scaled = dn * gain
        out = inv * scaled - x * (inv * inv * inv * jnp.mean(scaled * x, axis=1, keepdims=True))
        if j == 0:
            out = out + cots_ref[...].astype(F32)
        ret_ref[:, j] = out.reshape(ret_ref.shape[0], ret_ref.shape[2], width).astype(BF16)
    gain_out_ref[...] = gains


def sum_kernel(n_dev, slots, table_ref, back_ref, one_ref, out_ref, acc_ref):
    acc_ref[...] = jnp.zeros_like(acc_ref)

    def add(dest, carry):
        for slot in range(slots):
            block = table_ref[dest, slot]
            acc_ref[block] += back_ref[dest, slot].astype(F32)
        return carry

    lax.fori_loop(0, n_dev, add, 0, unroll=2)
    total = acc_ref[...].reshape(out_ref.shape).astype(BF16)
    out_ref[...] = nn(one_ref[0], total).astype(BF16)


VM = pl.BlockSpec(memory_space=pltpu.VMEM)
SM = pl.BlockSpec(memory_space=pltpu.SMEM)


def per_device(
    raster_tokens, hilbert_perm, neighbors, neighbor_counts, norm_gain, w_qkv, w_out, cotangent
):
    n_dev = lax.axis_size("ctx")
    me = lax.axis_index("ctx")
    rows, width = raster_tokens.shape
    slots = neighbors.shape[1]
    per_peer = rows // n_dev
    norm_scale = (rows * n_dev) ** (-0.5)
    n_rows = slots * BLOCK
    fits = per_peer % 8 == 0
    note = jnp.concatenate([hilbert_perm, jnp.pad(neighbors[0], (0, rows - slots))])
    note = jnp.broadcast_to(note[None, None], (n_dev, 1, 2 * rows))
    note = lax.all_to_all(note, "ctx", 0, 0, tiled=True)[:, 0]
    perm_all = note[:, :rows]
    table = note[:, rows:rows + slots]

    msg_shape = (n_dev, 1, slots, per_peer, width)
    if not fits:
        msg_shape = (1, 1, 1, 8, LANES)
    sort_shape = (1, n_dev, per_peer, width) if fits else (1, rows, width)
    msg, one, in_order = pl.pallas_call(
        functools.partial(pack_kernel, n_dev, slots, per_peer),
        out_shape=(
            jax.ShapeDtypeStruct(msg_shape, BF16),
            jax.ShapeDtypeStruct((1, rows, rows), BF16),
            jax.ShapeDtypeStruct(sort_shape, F32 if fits else BF16),
        ),
        in_specs=[SM, SM, VM, VM],
        out_specs=(VM, VM, VM),
    )(me[None], table, perm_all, raster_tokens[None])
    if not fits:
        msg = in_order.reshape(n_dev, per_peer, width)[table][:, None]
    msg = msg[:, 0]
    arrived = lax.all_to_all(msg, "ctx", 0, 0, tiled=True)
    if not fits:
        arrived = arrived.transpose(1, 0, 2, 3).reshape(1, slots, rows, width).transpose(0, 1, 2, 3)
        ret_shape = (1, slots, rows, width)
    else:
        ret_shape = (n_dev, slots, per_peer, width)

    layer_out, ret, gains, att, cots = pl.pallas_call(
        main_kernel,
        out_shape=(
            jax.ShapeDtypeStruct((rows, width), BF16),
            jax.ShapeDtypeStruct(ret_shape, BF16),
            jax.ShapeDtypeStruct((1, width), F32),
            jax.ShapeDtypeStruct((rows, width), BF16),
            jax.ShapeDtypeStruct((rows, width), BF16),
        ),
        in_specs=[SM] + [VM] * 6,
        out_specs=(VM,) * 5,
        scratch_shapes=[
            pltpu.VMEM((n_rows, width), F32),
            pltpu.VMEM((n_rows, LANES), F32),
            pltpu.VMEM((n_rows, width), BF16),
            pltpu.VMEM((rows, width), BF16),
            pltpu.VMEM((n_rows, 2 * width), BF16),
            pltpu.VMEM((rows, width), BF16),
            pltpu.VMEM((rows, width), F32),
            pltpu.VMEM((rows, width), BF16),
            pltpu.VMEM((n_rows, 2 * width), BF16),
        ],
    )(neighbor_counts, arrived, hilbert_perm[None], norm_gain[None], cotangent, w_qkv, w_out)

    grad_w_out = (
        lax.psum_scatter(tn(att, cots), "ctx", scatter_dimension=0, tiled=True) * norm_scale
    )
    high = gains.astype(BF16)
    low = (gains - high.astype(F32)).astype(BF16)
    extra = jnp.concatenate([high, low, jnp.zeros((6, width), BF16)])
    if fits:
        extra = jnp.broadcast_to(extra.reshape(1, 1, 8, width), (n_dev, 1, 8, width))
        back = lax.all_to_all(jnp.concatenate([ret, extra], axis=1), "ctx", 0, 0, tiled=True)
        parts = back[:, slots, :2].astype(F32)
        grad_tokens = pl.pallas_call(
            functools.partial(sum_kernel, n_dev, slots),
            out_shape=jax.ShapeDtypeStruct((rows, width), BF16),
            in_specs=[SM, VM, VM],
            out_specs=VM,
            scratch_shapes=[pltpu.VMEM((n_dev, per_peer, width), F32)],
        )(table, back, one)
    else:
        ret = ret.reshape(slots, n_dev, per_peer, width).transpose(1, 0, 2, 3)
        ret = ret.reshape(n_dev, slots * per_peer, width)
        extra = jnp.broadcast_to(extra[None, :2], (n_dev, 2, width))
        back = lax.all_to_all(jnp.concatenate([ret, extra], axis=1), "ctx", 0, 0, tiled=True)
        parts = back[:, slots * per_peer:].astype(F32)
        rest = back[:, :slots * per_peer].reshape(n_dev * slots, per_peer, width).astype(F32)
        total = jnp.zeros((n_dev, per_peer, width), F32).at[table.reshape(-1)].add(rest)
        grad_tokens = nn(one[0], total.reshape(rows, width).astype(BF16)).astype(BF16)
    grad_gain = jnp.sum(parts, axis=(0, 1)) * norm_scale
    return (layer_out, grad_tokens, grad_w_out, grad_gain)


def solution(mesh):
    placed = (
        P(("groups", "ctx"), None),
        P(("groups", "ctx")),
        P(("groups", "ctx"), None),
        P(("groups", "ctx")),
        P(),
        P(),
        P(),
        P(("groups", "ctx"), None),
    )
    return jax.shard_map(
        per_device,
        mesh=mesh,
        in_specs=placed,
        out_specs=(
            P(("groups", "ctx"), None),
            P(("groups", "ctx"), None),
            P(("groups", "ctx"), None),
            P("groups"),
        ),
        check_vma=False,
    )
```

```python
import functools

import jax
import jax.numpy as jnp
from jax import lax
from jax.experimental import pallas as pl
from jax.experimental.pallas import tpu as pltpu
from jax.sharding import PartitionSpec as P

HEADS = 16
BLOCK = 128
LANES = 128
EPS = 1e-06
FAR = -1e30
F32 = jnp.float32
BF16 = jnp.bfloat16


def iota(shape, dim):
    return lax.broadcasted_iota(jnp.int32, shape, dim)


def nn(a, b):
    return jnp.dot(a, b, preferred_element_type=F32)


def nt(a, b):
    return lax.dot_general(a, b, (((1,), (1,)), ((), ())), preferred_element_type=F32)


def tn(a, b):
    return lax.dot_general(a, b, (((0,), (0,)), ((), ())), preferred_element_type=F32)


def ranks(key_col, key_row, dim):
    if dim == 0:
        return jnp.sum((key_col < key_row).astype(F32), axis=0, keepdims=True).astype(jnp.int32)
    return jnp.sum((key_row < key_col).astype(F32), axis=1, keepdims=True).astype(jnp.int32)


def column_of(row):
    n = row.shape[1]
    wide = jnp.broadcast_to(row.astype(F32), (n, n))
    return jnp.transpose(wide)[:, :1].astype(jnp.int32)


def row_of(col):
    n = col.shape[0]
    wide = jnp.broadcast_to(col.astype(F32), (n, n))
    return jnp.transpose(wide)[:1, :].astype(jnp.int32)


def pack_kernel(n_dev, slots, per_peer, place_ref, table_ref, note_ref, own_ref, mirror_ref, msg_ref, one_ref, sorted_ref):
    rows, width = own_ref.shape
    half = n_dev // 2
    upper, seat = place_ref[0], place_ref[1]
    for part in range(2):
        target = (part * half + seat) * rows + iota((rows, 1), 0)

        def hit(block, acc):
            line = note_ref[block][:, :rows]
            return acc + jnp.where(line == target, block, 0)

        found = lax.fori_loop(0, n_dev, hit, jnp.zeros((rows, rows), jnp.int32), unroll=4)
        home = jnp.sum(found.astype(F32), axis=1, keepdims=True).astype(jnp.int32)
        key_col = home * rows + iota((rows, 1), 0)
        key_row = row_of(key_col)
        slot_row = ranks(key_col, key_row, 0)
        slot_col = ranks(key_col, key_row, 1)
        pick = (slot_row == iota((rows, rows), 0)).astype(BF16)
        one_ref[part] = (slot_col == iota((rows, rows), 1)).astype(BF16)
        chunk = jnp.where(upper == part, own_ref[...], mirror_ref[...])
        ordered = nn(pick, chunk)
        if per_peer % 8 == 0:
            sorted_ref[part] = ordered.reshape(n_dev, per_peer, width).astype(BF16)
        else:
            sorted_ref[part] = ordered.astype(BF16)
    if per_peer % 8 == 0:

        def place(dest, carry):
            for slot in range(slots):
                block = table_ref[upper * half + dest, 0, rows + slot]
                for part in range(2):
                    msg_ref[dest, part, slot] = sorted_ref[part, block]
            return carry

        lax.fori_loop(0, half, place, 0, unroll=2)


def main_kernel(
    fits, count_ref, arrived_ref, perm_ref, gain_ref, cot_ref, wqkv_ref, wout_ref,
    layer_ref, ret_ref, *rest
):
    if fits:
        x_ref, inv_ref, nrm_ref, q_ref, kv_ref, do_ref, attt_ref, cots_ref, dq_ref, dkv_ref = rest
    else:
        gain_out_ref, att_out_ref, x_ref, inv_ref, nrm_ref, q_ref, kv_ref, do_ref, attt_ref, cots_ref, dq_ref, dkv_ref = rest
    n_rows, width = x_ref.shape
    slots = n_rows // BLOCK
    head_dim = width // HEADS
    gain = gain_ref[...]
    key_row = perm_ref[...]
    key_col = column_of(key_row)
    slot_row = ranks(key_col, key_row, 0)
    slot_col = ranks(key_col, key_row, 1)
    to_arrival = (slot_row == iota((BLOCK, BLOCK), 0)).astype(BF16)
    to_order = (slot_col == iota((BLOCK, BLOCK), 1)).astype(BF16)
    cots_ref[...] = nn(to_arrival, cot_ref[...]).astype(BF16)
    for j in range(slots):
        if fits:
            part_rows = BLOCK // 2
            for part in range(2):
                x = arrived_ref[:, part, j].astype(F32).reshape(part_rows, width)
                x_ref[pl.ds(j * BLOCK + part * part_rows, part_rows), :] = x
        else:
            x_ref[pl.ds(j * BLOCK, BLOCK), :] = arrived_ref[j].astype(F32)
        x = x_ref[pl.ds(j * BLOCK, BLOCK), :]
        inv = lax.rsqrt(jnp.mean(x * x, axis=1, keepdims=True) + EPS)
        inv_ref[pl.ds(j * BLOCK, BLOCK), :] = jnp.broadcast_to(inv, (BLOCK, LANES))
        nrm_ref[pl.ds(j * BLOCK, BLOCK), :] = (x * inv * gain).astype(BF16)
    scale = head_dim ** (-0.5)
    q_ref[...] = nn(nrm_ref[pl.ds(0, BLOCK), :], wqkv_ref[:, :width]).astype(BF16)
    kv_ref[...] = nn(nrm_ref[...], wqkv_ref[:, width:]).astype(BF16)
    do_ref[...] = nt(cots_ref[...], wout_ref[...]).astype(BF16)
    count = count_ref[0]
    first = iota((BLOCK, LANES), 1) < head_dim

    def both(pair):
        zero = jnp.zeros_like(pair)
        return jnp.concatenate([jnp.where(first, pair, zero), jnp.where(first, zero, pair)], axis=0)

    def own(out):
        return jnp.concatenate([out[:head_dim, :BLOCK], out[head_dim:, BLOCK:]], axis=0)

    def pair_step(pair, carry):
        lane = pl.multiple_of(pair * LANES, LANES)
        cols = pl.ds(lane, LANES)
        vcols = pl.ds(pl.multiple_of(width + pair * LANES, LANES), LANES)
        qm = both(q_ref[:, cols])
        dom = both(do_ref[:, cols])
        k = kv_ref[:, cols]
        v = kv_ref[:, vcols]
        s = nt(k, qm) * scale
        s = jnp.concatenate(
            [jnp.where(j < count, s[j * BLOCK:(j + 1) * BLOCK], FAR) for j in range(slots)], axis=0
        )
        e = jnp.exp(s - jnp.max(s, axis=0, keepdims=True))
        p = e / jnp.sum(e, axis=0, keepdims=True)
        pb = p.astype(BF16)
        dp = nt(v, dom)
        dots = jnp.sum(dp * p, axis=0, keepdims=True)
        ds = (p * (dp - dots) * scale).astype(BF16)
        attt_ref[cols, :] = own(tn(v, pb)).astype(BF16)
        dq_ref[:, cols] = jnp.transpose(own(tn(k, ds))).astype(BF16)
        dkv_ref[:, cols] = nn(ds, qm).astype(BF16)
        dkv_ref[:, vcols] = nn(pb, dom).astype(BF16)
        return carry

    lax.fori_loop(0, width // LANES, pair_step, 0)
    layer = (x_ref[pl.ds(0, BLOCK), :] + tn(attt_ref[...], wout_ref[...])).astype(BF16)
    layer_ref[...] = nn(to_order, layer).astype(BF16)
    att = nt(attt_ref[...], to_order).astype(BF16)
    lane_blocks = width // LANES
    gains = jnp.zeros((1, width), F32)
    for j in range(slots):
        rows = pl.ds(j * BLOCK, BLOCK)
        dn = nt(dkv_ref[rows, :], wqkv_ref[:, width:])
        if j == 0:
            dn = dn + nt(dq_ref[...], wqkv_ref[:, :width])
        x = x_ref[rows, :]
        inv = inv_ref[rows, :][:, :1]
        gains = gains + jnp.sum(dn * (x * inv), axis=0, keepdims=True)
        scaled = dn * gain
        out = inv * scaled - x * (inv * inv * inv * jnp.mean(scaled * x, axis=1, keepdims=True))
        if j == 0:
            out = out + cots_ref[...].astype(F32)
        if fits:
            n_dev = ret_ref.shape[0]
            for lb in range(lane_blocks):
                piece = out[:, lb * LANES:(lb + 1) * LANES].reshape(n_dev, 8, LANES)
                ret_ref[:, pl.ds((j * lane_blocks + lb) * 8, 8), :] = piece.astype(BF16)
        else:
            ret_ref[j] = out.astype(BF16)
    if not fits:
        gain_out_ref[...] = gains
        att_out_ref[...] = att
        return
    base = slots * lane_blocks * 8
    feats = width // n_dev
    ret_ref[:, pl.ds(base, feats), :] = att.reshape(n_dev, feats, LANES)
    high = gains.astype(BF16).astype(F32)
    low = gains - high
    row = iota((8, LANES), 0)
    for part, value in enumerate((high, low)):
        tile = jnp.zeros((8, LANES), F32)
        for lb in range(lane_blocks):
            tile = jnp.where(row == lb, value[:, lb * LANES:(lb + 1) * LANES], tile)
        tile = jnp.broadcast_to(tile.astype(BF16)[None], (n_dev, 8, LANES))
        ret_ref[:, pl.ds(base + feats + part * 8, 8), :] = tile


def finish_kernel(
    n_dev, slots, masks, norm_scale, place_ref, table_ref, back_ref, one_ref, *rest
):
    cots = rest[:len(masks)]
    out_ref, gw_ref, gain_ref, acc_ref = rest[len(masks):]
    rows, width = out_ref.shape
    lane_blocks = width // LANES
    size = lane_blocks * 8
    acc_ref[...] = jnp.zeros_like(acc_ref)

    def add(dest, carry):
        for slot in range(slots):
            block = table_ref[dest, 0, rows + slot]
            acc_ref[block] += back_ref[dest, pl.ds(slot * size, size), :].astype(F32)
        return carry

    lax.fori_loop(0, n_dev, add, 0, unroll=2)
    upper, seat = place_ref[0], place_ref[1]
    me = upper * (n_dev // 2) + seat
    one = one_ref[upper]
    for lb in range(lane_blocks):
        total = acc_ref[:, pl.ds(lb * 8, 8), :].reshape(rows, LANES).astype(BF16)
        out_ref[:, pl.ds(lb * LANES, LANES)] = nn(one, total).astype(BF16)
    base = slots * size
    feats = width // n_dev
    acc = jnp.zeros((feats, width), F32)
    for group, ref in zip(masks, cots):
        for at, mask in enumerate(group):
            att = back_ref[me ^ mask, pl.ds(base, feats), :]
            acc = acc + nn(att, ref[pl.ds(at * rows, rows), :])
    gw_ref[...] = acc * norm_scale
    tile = jnp.zeros((8, LANES), F32)
    for dest in range(n_dev):
        for part in range(2):
            tile = tile + back_ref[dest, pl.ds(base + feats + part * 8, 8), :].astype(F32)
    gain_ref[...] = tile * norm_scale


VM = pl.BlockSpec(memory_space=pltpu.VMEM)
SM = pl.BlockSpec(memory_space=pltpu.SMEM)


def swap(block, mask):
    n_dev = lax.axis_size("ctx")
    return lax.ppermute(block, "ctx", [(i, i ^ mask) for i in range(n_dev)])


def gather_cotangent(cotangent, n_dev):
    masks = [2, n_dev // 2]
    masks += [m for m in (1 << b for b in range(n_dev.bit_length() - 1)) if m not in masks + [1]]
    held, names = cotangent, [0]
    for mask in masks[:-1]:
        other = swap(held, mask)
        held = jnp.concatenate([held, other])
        names = names + [m ^ mask for m in names]
    other = swap(held, masks[-1])
    others = [m ^ masks[-1] for m in names]
    pieces = [(names, held), (others, other)]
    return pieces + [([m ^ 1 for m in group], swap(piece, 1)) for group, piece in pieces]


def per_device(
    raster_tokens, hilbert_perm, neighbors, neighbor_counts, norm_gain, w_qkv, w_out, cotangent
):
    n_dev = lax.axis_size("ctx")
    half = n_dev // 2
    me = lax.axis_index("ctx")
    rows, width = raster_tokens.shape
    slots = neighbors.shape[1]
    per_peer = rows // n_dev
    norm_scale = (rows * n_dev) ** (-0.5)
    n_rows = slots * BLOCK
    fits = per_peer % 8 == 0
    lane_blocks = width // LANES
    feats = width // n_dev
    place = jnp.stack([me // half, me % half]).astype(jnp.int32)
    note = jnp.concatenate([hilbert_perm, jnp.pad(neighbors[0], (0, rows - slots))])
    note = jnp.broadcast_to(note[None, None], (n_dev, 1, 2 * rows))
    mirror = swap(raster_tokens, half)
    pieces = gather_cotangent(cotangent, n_dev)
    note = lax.all_to_all(note, "ctx", 0, 0, tiled=True)

    msg_shape = (half, 2, slots, per_peer, width) if fits else (8, LANES)
    sort_shape = (2, n_dev, per_peer, width) if fits else (2, rows, width)
    msg, one, in_order = pl.pallas_call(
        functools.partial(pack_kernel, n_dev, slots, per_peer),
        out_shape=(
            jax.ShapeDtypeStruct(msg_shape, BF16),
            jax.ShapeDtypeStruct((2, rows, rows), BF16),
            jax.ShapeDtypeStruct(sort_shape, BF16),
        ),
        in_specs=[SM, SM, VM, VM, VM],
        out_specs=(VM, VM, VM),
    )(place, note, note, raster_tokens, mirror)
    table = note[:, 0, rows:rows + slots]
    if not fits:
        mine = lax.dynamic_slice_in_dim(table, place[0] * half, half, 0)
        msg = in_order.reshape(2, n_dev, per_peer, width)[:, mine].transpose(1, 0, 2, 3, 4)
    halves = [list(range(half)), list(range(half, n_dev))]
    arrived = lax.all_to_all(msg, "ctx", 0, 0, tiled=True, axis_index_groups=halves)
    if fits:
        ret_shape = (n_dev, slots * lane_blocks * 8 + feats + 16, LANES)
        extra_shapes = ()
    else:
        arrived = arrived.transpose(2, 1, 0, 3, 4).reshape(slots, rows, width)
        ret_shape = (slots, rows, width)
        extra_shapes = (
            jax.ShapeDtypeStruct((1, width), F32),
            jax.ShapeDtypeStruct((width, rows), BF16),
        )

    layer_out, ret, *extra = pl.pallas_call(
        functools.partial(main_kernel, fits),
        out_shape=(
            jax.ShapeDtypeStruct((rows, width), BF16),
            jax.ShapeDtypeStruct(ret_shape, BF16),
        ) + extra_shapes,
        in_specs=[SM] + [VM] * 6,
        out_specs=(VM,) * (2 + len(extra_shapes)),
        scratch_shapes=[
            pltpu.VMEM((n_rows, width), F32),
            pltpu.VMEM((n_rows, LANES), F32),
            pltpu.VMEM((n_rows, width), BF16),
            pltpu.VMEM((rows, width), BF16),
            pltpu.VMEM((n_rows, 2 * width), BF16),
            pltpu.VMEM((rows, width), BF16),
            pltpu.VMEM((width, rows), BF16),
            pltpu.VMEM((rows, width), BF16),
            pltpu.VMEM((rows, width), BF16),
            pltpu.VMEM((n_rows, 2 * width), BF16),
        ],
        cost_estimate=pl.CostEstimate(
            flops=14 * n_rows * width * width, bytes_accessed=16 * width * width, transcendentals=0
        ),
    )(neighbor_counts, arrived, hilbert_perm[None], norm_gain[None], cotangent, w_qkv, w_out)

    if fits:
        back = lax.all_to_all(ret, "ctx", 0, 0, tiled=True)
        masks = [group for group, piece in pieces]
        grad_tokens, grad_w_out, grad_gain = pl.pallas_call(
            functools.partial(finish_kernel, n_dev, slots, masks, norm_scale),
            out_shape=(
                jax.ShapeDtypeStruct((rows, width), BF16),
                jax.ShapeDtypeStruct((feats, width), F32),
                jax.ShapeDtypeStruct((lane_blocks, LANES), F32),
            ),
            in_specs=[SM, SM, VM, VM] + [VM] * len(pieces),
            out_specs=(VM, VM, VM),
            scratch_shapes=[pltpu.VMEM((n_dev, lane_blocks * 8, LANES), F32)],
        )(place, note, back, one, *[piece for group, piece in pieces])
        return (layer_out, grad_tokens, grad_w_out, grad_gain.reshape(width))
    gains, att = extra
    high = gains.astype(BF16)
    low = (gains - high.astype(F32)).astype(BF16)
    ret = ret.reshape(slots, n_dev, per_peer, width).transpose(1, 0, 2, 3).reshape(n_dev, -1)
    both = jnp.broadcast_to(jnp.concatenate([high, low]).reshape(1, -1), (n_dev, 2 * width))
    sizes = (ret.shape[1], feats * rows)
    ret = jnp.concatenate([ret, att.reshape(n_dev, -1), both], axis=1).reshape(n_dev, -1, LANES)
    back = lax.all_to_all(ret, "ctx", 0, 0, tiled=True).reshape(n_dev, -1)
    rest = back[:, :sizes[0]].reshape(n_dev * slots, per_peer, width).astype(F32)
    total = jnp.zeros((n_dev, per_peer, width), F32).at[table.reshape(-1)].add(rest)
    grad_tokens = nn(one[place[0]], total.reshape(rows, width).astype(BF16)).astype(BF16)
    att = back[:, sizes[0]:sizes[0] + sizes[1]].reshape(n_dev, feats, rows)
    order = me ^ jnp.array(sum([group for group, piece in pieces], []))
    cots = jnp.concatenate([piece for group, piece in pieces]).reshape(n_dev, rows, width)
    grad_w_out = jnp.einsum("sft,stw->fw", att[order], cots, preferred_element_type=F32) * norm_scale
    parts = back[:, sizes[0] + sizes[1]:].reshape(n_dev, 2, width).astype(F32)
    grad_gain = jnp.sum(parts, axis=(0, 1)) * norm_scale
    return (layer_out, grad_tokens, grad_w_out, grad_gain)


def solution(mesh):
    placed = (
        P(("groups", "ctx"), None),
        P(("groups", "ctx")),
        P(("groups", "ctx"), None),
        P(("groups", "ctx")),
        P(),
        P(),
        P(),
        P(("groups", "ctx"), None),
    )
    return jax.shard_map(
        per_device,
        mesh=mesh,
        in_specs=placed,
        out_specs=(
            P(("groups", "ctx"), None),
            P(("groups", "ctx"), None),
            P(("groups", "ctx"), None),
            P("groups"),
        ),
        check_vma=False,
    )
```

```python
import functools

import jax
import jax.numpy as jnp
from jax import lax
from jax.experimental import pallas as pl
from jax.experimental.pallas import tpu as pltpu
from jax.sharding import PartitionSpec as P


HEADS = 16
BLOCK = 128
LANES = 128
EPS = 1e-06
FAR = -1e30
F32 = jnp.float32
BF16 = jnp.bfloat16


def iota(shape, dim):
    return lax.broadcasted_iota(jnp.int32, shape, dim)


def nn(a, b):
    return jnp.dot(a, b, preferred_element_type=F32)


def nt(a, b):
    return lax.dot_general(a, b, (((1,), (1,)), ((), ())), preferred_element_type=F32)


def tn(a, b):
    return lax.dot_general(a, b, (((0,), (0,)), ((), ())), preferred_element_type=F32)


def ranks(key_col, key_row, dim):
    if dim == 0:
        return jnp.sum((key_col < key_row).astype(F32), axis=0, keepdims=True).astype(jnp.int32)
    return jnp.sum((key_row < key_col).astype(F32), axis=1, keepdims=True).astype(jnp.int32)


def column_of(row):
    n = row.shape[1]
    wide = jnp.broadcast_to(row.astype(F32), (n, n))
    return jnp.transpose(wide)[:, :1].astype(jnp.int32)


def row_of(col):
    n = col.shape[0]
    wide = jnp.broadcast_to(col.astype(F32), (n, n))
    return jnp.transpose(wide)[:1, :].astype(jnp.int32)


def pack_kernel(n_dev, slots, per_peer, place_ref, table_ref, note_ref, own_ref, mirror_ref, cot_ref, other_ref, msg_ref, one_ref, sorted_ref, held_ref):
    held_ref[pl.ds(0, cot_ref.shape[0]), :] = cot_ref[...]
    held_ref[pl.ds(cot_ref.shape[0], cot_ref.shape[0]), :] = other_ref[...]
    rows, width = own_ref.shape
    half = n_dev // 2
    upper, seat = place_ref[0], place_ref[1]
    for part in range(2):
        target = (part * half + seat) * rows + iota((rows, 1), 0)

        def hit(block, acc):
            line = note_ref[block][:, :rows]
            return acc + jnp.where(line == target, block, 0)

        found = lax.fori_loop(0, n_dev, hit, jnp.zeros((rows, rows), jnp.int32), unroll=4)
        home = jnp.sum(found.astype(F32), axis=1, keepdims=True).astype(jnp.int32)
        key_col = home * rows + iota((rows, 1), 0)
        key_row = row_of(key_col)
        slot_row = ranks(key_col, key_row, 0)
        slot_col = ranks(key_col, key_row, 1)
        pick = (slot_row == iota((rows, rows), 0)).astype(BF16)
        one_ref[part] = (slot_col == iota((rows, rows), 1)).astype(BF16)
        chunk = jnp.where(upper == part, own_ref[...], mirror_ref[...])
        ordered = nn(pick, chunk)
        if per_peer % 8 == 0:
            sorted_ref[part] = ordered.reshape(n_dev, per_peer, width).astype(BF16)
        else:
            sorted_ref[part] = ordered.astype(BF16)
    if per_peer % 8 == 0:

        def place(dest, carry):
            for slot in range(slots):
                block = table_ref[upper * half + dest, 0, rows + slot]
                for part in range(2):
                    msg_ref[dest, part, slot] = sorted_ref[part, block]
            return carry

        lax.fori_loop(0, half, place, 0, unroll=2)


def main_kernel(
    fits, count_ref, arrived_ref, perm_ref, gain_ref, cot_ref, wqkv_ref, wout_ref,
    layer_ref, ret_ref, *rest
):
    if fits:
        x_ref, inv_ref, nrm_ref, q_ref, kv_ref, do_ref, attt_ref, cots_ref, dq_ref, dkv_ref = rest
    else:
        gain_out_ref, att_out_ref, x_ref, inv_ref, nrm_ref, q_ref, kv_ref, do_ref, attt_ref, cots_ref, dq_ref, dkv_ref = rest
    n_rows, width = x_ref.shape
    slots = n_rows // BLOCK
    head_dim = width // HEADS
    gain = gain_ref[...]
    key_row = perm_ref[...]
    key_col = column_of(key_row)
    slot_row = ranks(key_col, key_row, 0)
    slot_col = ranks(key_col, key_row, 1)
    to_arrival = (slot_row == iota((BLOCK, BLOCK), 0)).astype(BF16)
    to_order = (slot_col == iota((BLOCK, BLOCK), 1)).astype(BF16)
    cots_ref[...] = nn(to_arrival, cot_ref[...]).astype(BF16)
    for j in range(slots):
        if fits:
            part_rows = BLOCK // 2
            for part in range(2):
                x = arrived_ref[:, part, j].astype(F32).reshape(part_rows, width)
                x_ref[pl.ds(j * BLOCK + part * part_rows, part_rows), :] = x
        else:
            x_ref[pl.ds(j * BLOCK, BLOCK), :] = arrived_ref[j].astype(F32)
        x = x_ref[pl.ds(j * BLOCK, BLOCK), :]
        inv = lax.rsqrt(jnp.mean(x * x, axis=1, keepdims=True) + EPS)
        inv_ref[pl.ds(j * BLOCK, BLOCK), :] = jnp.broadcast_to(inv, (BLOCK, LANES))
        nrm_ref[pl.ds(j * BLOCK, BLOCK), :] = (x * inv * gain).astype(BF16)
    scale = head_dim ** (-0.5)
    q_ref[...] = nn(nrm_ref[pl.ds(0, BLOCK), :], wqkv_ref[:, :width]).astype(BF16)
    kv_ref[...] = nn(nrm_ref[...], wqkv_ref[:, width:]).astype(BF16)
    do_ref[...] = nt(cots_ref[...], wout_ref[...]).astype(BF16)
    count = count_ref[0]
    first = iota((BLOCK, LANES), 1) < head_dim

    def both(pair):
        zero = jnp.zeros_like(pair)
        return jnp.concatenate([jnp.where(first, pair, zero), jnp.where(first, zero, pair)], axis=0)

    def own(out):
        return jnp.concatenate([out[:head_dim, :BLOCK], out[head_dim:, BLOCK:]], axis=0)

    def pair_step(pair, carry):
        lane = pl.multiple_of(pair * LANES, LANES)
        cols = pl.ds(lane, LANES)
        vcols = pl.ds(pl.multiple_of(width + pair * LANES, LANES), LANES)
        qm = both(q_ref[:, cols])
        dom = both(do_ref[:, cols])
        k = kv_ref[:, cols]
        v = kv_ref[:, vcols]
        s = nt(k, qm) * scale
        s = jnp.concatenate(
            [jnp.where(j < count, s[j * BLOCK:(j + 1) * BLOCK], FAR) for j in range(slots)], axis=0
        )
        e = jnp.exp(s - jnp.max(s, axis=0, keepdims=True))
        p = e / jnp.sum(e, axis=0, keepdims=True)
        pb = p.astype(BF16)
        dp = nt(v, dom)
        dots = jnp.sum(dp * p, axis=0, keepdims=True)
        ds = (p * (dp - dots) * scale).astype(BF16)
        attt_ref[cols, :] = own(tn(v, pb)).astype(BF16)
        dq_ref[:, cols] = jnp.transpose(own(tn(k, ds))).astype(BF16)
        dkv_ref[:, cols] = nn(ds, qm).astype(BF16)
        dkv_ref[:, vcols] = nn(pb, dom).astype(BF16)
        return carry

    lax.fori_loop(0, width // LANES, pair_step, 0)
    layer = (x_ref[pl.ds(0, BLOCK), :] + tn(attt_ref[...], wout_ref[...])).astype(BF16)
    layer_ref[...] = nn(to_order, layer).astype(BF16)
    att = nt(attt_ref[...], to_order).astype(BF16)
    lane_blocks = width // LANES
    gains = jnp.zeros((1, width), F32)
    for j in range(slots):
        rows = pl.ds(j * BLOCK, BLOCK)
        dn = nt(dkv_ref[rows, :], wqkv_ref[:, width:])
        if j == 0:
            dn = dn + nt(dq_ref[...], wqkv_ref[:, :width])
        x = x_ref[rows, :]
        inv = inv_ref[rows, :][:, :1]
        gains = gains + jnp.sum(dn * (x * inv), axis=0, keepdims=True)
        scaled = dn * gain
        out = inv * scaled - x * (inv * inv * inv * jnp.mean(scaled * x, axis=1, keepdims=True))
        if j == 0:
            out = out + cots_ref[...].astype(F32)
        if fits:
            n_dev = ret_ref.shape[0]
            for lb in range(lane_blocks):
                piece = out[:, lb * LANES:(lb + 1) * LANES].reshape(n_dev, 8, LANES)
                ret_ref[:, pl.ds((j * lane_blocks + lb) * 8, 8), :] = piece.astype(BF16)
        else:
            ret_ref[j] = out.astype(BF16)
    if not fits:
        gain_out_ref[...] = gains
        att_out_ref[...] = att
        return
    base = slots * lane_blocks * 8
    feats = width // n_dev
    ret_ref[:, pl.ds(base, feats), :] = att.reshape(n_dev, feats, LANES)
    high = gains.astype(BF16).astype(F32)
    low = gains - high
    row = iota((8, LANES), 0)
    for part, value in enumerate((high, low)):
        tile = jnp.zeros((8, LANES), F32)
        for lb in range(lane_blocks):
            tile = jnp.where(row == lb, value[:, lb * LANES:(lb + 1) * LANES], tile)
        tile = jnp.broadcast_to(tile.astype(BF16)[None], (n_dev, 8, LANES))
        ret_ref[:, pl.ds(base + feats + part * 8, 8), :] = tile


def finish_kernel(
    n_dev, slots, masks, norm_scale, place_ref, table_ref, back_ref, one_ref, *rest
):
    cots = rest[:len(masks)]
    out_ref, gw_ref, gain_ref, acc_ref = rest[len(masks):]
    rows, width = out_ref.shape
    lane_blocks = width // LANES
    size = lane_blocks * 8
    acc_ref[...] = jnp.zeros_like(acc_ref)

    def add(dest, carry):
        for slot in range(slots):
            block = table_ref[dest, 0, rows + slot]
            acc_ref[block] += back_ref[dest, pl.ds(slot * size, size), :].astype(F32)
        return carry

    lax.fori_loop(0, n_dev, add, 0, unroll=2)
    upper, seat = place_ref[0], place_ref[1]
    me = upper * (n_dev // 2) + seat
    one = one_ref[upper]
    for lb in range(lane_blocks):
        total = acc_ref[:, pl.ds(lb * 8, 8), :].reshape(rows, LANES).astype(BF16)
        out_ref[:, pl.ds(lb * LANES, LANES)] = nn(one, total).astype(BF16)
    base = slots * size
    feats = width // n_dev
    acc = jnp.zeros((feats, width), F32)
    for group, ref in zip(masks, cots):
        for at, mask in enumerate(group):
            att = back_ref[me ^ mask, pl.ds(base, feats), :]
            acc = acc + nn(att, ref[pl.ds(at * rows, rows), :])
    gw_ref[...] = acc * norm_scale
    tile = jnp.zeros((8, LANES), F32)
    for dest in range(n_dev):
        for part in range(2):
            tile = tile + back_ref[dest, pl.ds(base + feats + part * 8, 8), :].astype(F32)
    gain_ref[...] = tile * norm_scale


VM = pl.BlockSpec(memory_space=pltpu.VMEM)
SM = pl.BlockSpec(memory_space=pltpu.SMEM)


def swap(block, mask):
    n_dev = lax.axis_size("ctx")
    return lax.ppermute(block, "ctx", [(i, i ^ mask) for i in range(n_dev)])


def per_device(
    raster_tokens, hilbert_perm, neighbors, neighbor_counts, norm_gain, w_qkv, w_out, cotangent
):
    n_dev = lax.axis_size("ctx")
    half = n_dev // 2
    me = lax.axis_index("ctx")
    rows, width = raster_tokens.shape
    slots = neighbors.shape[1]
    per_peer = rows // n_dev
    norm_scale = (rows * n_dev) ** (-0.5)
    n_rows = slots * BLOCK
    fits = per_peer % 8 == 0
    lane_blocks = width // LANES
    feats = width // n_dev
    place = jnp.stack([me // half, me % half]).astype(jnp.int32)
    note = jnp.concatenate([hilbert_perm, jnp.pad(neighbors[0], (0, rows - slots))])
    note = jnp.broadcast_to(note[None, None], (n_dev, 1, 2 * rows))
    mirror = swap(raster_tokens, half)
    other = swap(cotangent, half // 2)
    note = lax.all_to_all(note, "ctx", 0, 0, tiled=True)
    note, other = lax.optimization_barrier((note, other))

    msg_shape = (half, 2, slots, per_peer, width) if fits else (8, LANES)
    sort_shape = (2, n_dev, per_peer, width) if fits else (2, rows, width)
    msg, one, in_order, held = pl.pallas_call(
        functools.partial(pack_kernel, n_dev, slots, per_peer),
        out_shape=(
            jax.ShapeDtypeStruct(msg_shape, BF16),
            jax.ShapeDtypeStruct((2, rows, rows), BF16),
            jax.ShapeDtypeStruct(sort_shape, BF16),
            jax.ShapeDtypeStruct((2 * rows, width), BF16),
        ),
        in_specs=[SM, SM] + [VM] * 5,
        out_specs=(VM,) * 4,
    )(place, note, note, raster_tokens, mirror, cotangent, other)
    table = note[:, 0, rows:rows + slots]
    if not fits:
        mine = lax.dynamic_slice_in_dim(table, place[0] * half, half, 0)
        msg = in_order.reshape(2, n_dev, per_peer, width)[:, mine].transpose(1, 0, 2, 3, 4)
    halves = [list(range(half)), list(range(half, n_dev))]
    arrived = lax.all_to_all(msg, "ctx", 0, 0, tiled=True, axis_index_groups=halves)
    arrived, held = lax.optimization_barrier((arrived, held))
    names = [0, half // 2]
    bits = [1 << b for b in range(n_dev.bit_length() - 1)]
    for mask in [m for m in bits if m not in (1, 2, half, half // 2)]:
        held = jnp.concatenate([held, swap(held, mask)])
        names = names + [m ^ mask for m in names]
    across = swap(held, half)
    beside = swap(held, 2)
    if fits:
        ret_shape = (n_dev, slots * lane_blocks * 8 + feats + 16, LANES)
        extra_shapes = ()
    else:
        arrived = arrived.transpose(2, 1, 0, 3, 4).reshape(slots, rows, width)
        ret_shape = (slots, rows, width)
        extra_shapes = (
            jax.ShapeDtypeStruct((1, width), F32),
            jax.ShapeDtypeStruct((width, rows), BF16),
        )

    layer_out, ret, *extra = pl.pallas_call(
        functools.partial(main_kernel, fits),
        out_shape=(
            jax.ShapeDtypeStruct((rows, width), BF16),
            jax.ShapeDtypeStruct(ret_shape, BF16),
        ) + extra_shapes,
        in_specs=[SM] + [VM] * 6,
        out_specs=(VM,) * (2 + len(extra_shapes)),
        scratch_shapes=[
            pltpu.VMEM((n_rows, width), F32),
            pltpu.VMEM((n_rows, LANES), F32),
            pltpu.VMEM((n_rows, width), BF16),
            pltpu.VMEM((rows, width), BF16),
            pltpu.VMEM((n_rows, 2 * width), BF16),
            pltpu.VMEM((rows, width), BF16),
            pltpu.VMEM((width, rows), BF16),
            pltpu.VMEM((rows, width), BF16),
            pltpu.VMEM((rows, width), BF16),
            pltpu.VMEM((n_rows, 2 * width), BF16),
        ],
        cost_estimate=pl.CostEstimate(
            flops=14 * n_rows * width * width, bytes_accessed=16 * width * width, transcendentals=0
        ),
    )(neighbor_counts, arrived, hilbert_perm[None], norm_gain[None], cotangent, w_qkv, w_out)

    if fits:
        ret, across, beside = lax.optimization_barrier((ret, across, beside))
        back = lax.all_to_all(ret, "ctx", 0, 0, tiled=True)
    corner = swap(across, 2)
    pieces = [
        (names, held),
        ([m ^ half for m in names], across),
        ([m ^ 2 for m in names], beside),
        ([m ^ 2 ^ half for m in names], corner),
    ]
    for group, piece in list(pieces):
        pieces.append(([m ^ 1 for m in group], swap(piece, 1)))
    if fits:
        masks = [group for group, piece in pieces]
        grad_tokens, grad_w_out, grad_gain = pl.pallas_call(
            functools.partial(finish_kernel, n_dev, slots, masks, norm_scale),
            out_shape=(
                jax.ShapeDtypeStruct((rows, width), BF16),
                jax.ShapeDtypeStruct((feats, width), F32),
                jax.ShapeDtypeStruct((lane_blocks, LANES), F32),
            ),
            in_specs=[SM, SM, VM, VM] + [VM] * len(pieces),
            out_specs=(VM, VM, VM),
            scratch_shapes=[pltpu.VMEM((n_dev, lane_blocks * 8, LANES), F32)],
        )(place, note, back, one, *[piece for group, piece in pieces])
        return (layer_out, grad_tokens, grad_w_out, grad_gain.reshape(width))
    gains, att = extra
    high = gains.astype(BF16)
    low = (gains - high.astype(F32)).astype(BF16)
    ret = ret.reshape(slots, n_dev, per_peer, width).transpose(1, 0, 2, 3).reshape(n_dev, -1)
    both = jnp.broadcast_to(jnp.concatenate([high, low]).reshape(1, -1), (n_dev, 2 * width))
    sizes = (ret.shape[1], feats * rows)
    ret = jnp.concatenate([ret, att.reshape(n_dev, -1), both], axis=1).reshape(n_dev, -1, LANES)
    back = lax.all_to_all(ret, "ctx", 0, 0, tiled=True).reshape(n_dev, -1)
    rest = back[:, :sizes[0]].reshape(n_dev * slots, per_peer, width).astype(F32)
    total = jnp.zeros((n_dev, per_peer, width), F32).at[table.reshape(-1)].add(rest)
    grad_tokens = nn(one[place[0]], total.reshape(rows, width).astype(BF16)).astype(BF16)
    att = back[:, sizes[0]:sizes[0] + sizes[1]].reshape(n_dev, feats, rows)
    order = me ^ jnp.array(sum([group for group, piece in pieces], []))
    cots = jnp.concatenate([piece for group, piece in pieces]).reshape(n_dev, rows, width)
    grad_w_out = jnp.einsum("sft,stw->fw", att[order], cots, preferred_element_type=F32) * norm_scale
    parts = back[:, sizes[0] + sizes[1]:].reshape(n_dev, 2, width).astype(F32)
    grad_gain = jnp.sum(parts, axis=(0, 1)) * norm_scale
    return (layer_out, grad_tokens, grad_w_out, grad_gain)


def solution(mesh):
    placed = (
        P(("groups", "ctx"), None),
        P(("groups", "ctx")),
        P(("groups", "ctx"), None),
        P(("groups", "ctx")),
        P(),
        P(),
        P(),
        P(("groups", "ctx"), None),
    )

    return jax.shard_map(
        per_device,
        mesh=mesh,
        in_specs=placed,
        out_specs=(
            P(("groups", "ctx"), None),
            P(("groups", "ctx"), None),
            P(("groups", "ctx"), None),
            P("groups"),
        ),
        check_vma=False,
    )
```

```python
import functools

import jax
import jax.numpy as jnp
from jax import lax
from jax.experimental import pallas as pl
from jax.experimental.pallas import tpu as pltpu
from jax.sharding import PartitionSpec as P


HEADS = 16
BLOCK = 128
LANES = 128
EPS = 1e-06
FAR = -1e30
F32 = jnp.float32
BF16 = jnp.bfloat16


def iota(shape, dim):
    return lax.broadcasted_iota(jnp.int32, shape, dim)


def nn(a, b):
    return jnp.dot(a, b, preferred_element_type=F32)


def nt(a, b):
    return lax.dot_general(a, b, (((1,), (1,)), ((), ())), preferred_element_type=F32)


def tn(a, b):
    return lax.dot_general(a, b, (((0,), (0,)), ((), ())), preferred_element_type=F32)


def ranks(key_col, key_row, dim):
    if dim == 0:
        return jnp.sum((key_col < key_row).astype(F32), axis=0, keepdims=True).astype(jnp.int32)
    return jnp.sum((key_row < key_col).astype(F32), axis=1, keepdims=True).astype(jnp.int32)


def column_of(row):
    n = row.shape[1]
    wide = jnp.broadcast_to(row.astype(F32), (n, n))
    return jnp.transpose(wide)[:, :1].astype(jnp.int32)


def row_of(col):
    n = col.shape[0]
    wide = jnp.broadcast_to(col.astype(F32), (n, n))
    return jnp.transpose(wide)[:1, :].astype(jnp.int32)


def pack_kernel(n_dev, slots, per_peer, place_ref, table_ref, note_ref, own_ref, mirror_ref, msg_ref, one_ref, sorted_ref):
    rows, width = own_ref.shape
    half = n_dev // 2
    upper, seat = place_ref[0], place_ref[1]
    for part in range(2):
        target = (part * half + seat) * rows + iota((rows, 1), 0)

        def hit(block, acc):
            line = note_ref[block][:, :rows]
            return acc + jnp.where(line == target, block, 0)

        found = lax.fori_loop(0, n_dev, hit, jnp.zeros((rows, rows), jnp.int32), unroll=4)
        home = jnp.sum(found.astype(F32), axis=1, keepdims=True).astype(jnp.int32)
        key_col = home * rows + iota((rows, 1), 0)
        key_row = row_of(key_col)
        slot_row = ranks(key_col, key_row, 0)
        slot_col = ranks(key_col, key_row, 1)
        pick = (slot_row == iota((rows, rows), 0)).astype(BF16)
        one_ref[part] = (slot_col == iota((rows, rows), 1)).astype(BF16)
        chunk = jnp.where(upper == part, own_ref[...], mirror_ref[...])
        ordered = nn(pick, chunk)
        if per_peer % 8 == 0:
            sorted_ref[part] = ordered.reshape(n_dev, per_peer, width).astype(BF16)
        else:
            sorted_ref[part] = ordered.astype(BF16)
    if per_peer % 8 == 0:

        def place(dest, carry):
            for slot in range(slots):
                block = table_ref[upper * half + dest, 0, rows + slot]
                for part in range(2):
                    msg_ref[dest, part, slot] = sorted_ref[part, block]
            return carry

        lax.fori_loop(0, half, place, 0, unroll=2)


def ready_kernel(
    cot_ref, other_ref, perm_ref, wout_ref, held_ref, cots_ref, do_ref, order_ref
):
    rows = cot_ref.shape[0]
    held_ref[pl.ds(0, rows), :] = cot_ref[...]
    held_ref[pl.ds(rows, rows), :] = other_ref[...]
    key_row = perm_ref[...]
    key_col = column_of(key_row)
    slot_row = ranks(key_col, key_row, 0)
    slot_col = ranks(key_col, key_row, 1)
    to_arrival = (slot_row == iota((BLOCK, BLOCK), 0)).astype(BF16)
    order_ref[...] = (slot_col == iota((BLOCK, BLOCK), 1)).astype(BF16)
    cots_ref[...] = nn(to_arrival, cot_ref[...]).astype(BF16)
    do_ref[...] = nt(cots_ref[...], wout_ref[...]).astype(BF16)


def main_kernel(
    fits, count_ref, arrived_ref, order_ref, gain_ref, cots_ref, do_ref, wqkv_hbm, wout_hbm,
    layer_ref, ret_ref, *rest
):
    if fits:
        x_ref, inv_ref, nrm_ref, q_ref, kv_ref, attt_ref, dq_ref, dkv_ref, dn_ref, wqkv_ref, wout_ref, sems = rest
    else:
        gain_out_ref, att_out_ref, x_ref, inv_ref, nrm_ref, q_ref, kv_ref, attt_ref, dq_ref, dkv_ref, dn_ref, wqkv_ref, wout_ref, sems = rest
    n_rows, width = x_ref.shape
    slots = n_rows // BLOCK
    head_dim = width // HEADS
    gain = gain_ref[...]
    to_order = order_ref[...]
    loads = []
    for at, (start, size) in enumerate(((width, width), (2 * width, width), (0, width))):
        part = pl.ds(start, size)
        loads.append(pltpu.make_async_copy(wqkv_hbm.at[:, part], wqkv_ref.at[:, part], sems.at[at]))
    loads.append(pltpu.make_async_copy(wout_hbm, wout_ref, sems.at[3]))
    for load in loads:
        load.start()
    for j in range(slots):
        if fits:
            part_rows = BLOCK // 2
            for part in range(2):
                x = arrived_ref[:, part, j].astype(F32).reshape(part_rows, width)
                x_ref[pl.ds(j * BLOCK + part * part_rows, part_rows), :] = x
        else:
            x_ref[pl.ds(j * BLOCK, BLOCK), :] = arrived_ref[j].astype(F32)
        x = x_ref[pl.ds(j * BLOCK, BLOCK), :]
        inv = lax.rsqrt(jnp.mean(x * x, axis=1, keepdims=True) + EPS)
        inv_ref[pl.ds(j * BLOCK, BLOCK), :] = jnp.broadcast_to(inv, (BLOCK, LANES))
        nrm_ref[pl.ds(j * BLOCK, BLOCK), :] = (x * inv * gain).astype(BF16)
    scale = head_dim ** (-0.5)
    for at in range(2):
        loads[at].wait()
        weight = wqkv_ref[:, (at + 1) * width:(at + 2) * width]
        kv_ref[:, pl.ds(at * width, width)] = nn(nrm_ref[...], weight).astype(BF16)
    loads[2].wait()
    q_ref[...] = nn(nrm_ref[pl.ds(0, BLOCK), :], wqkv_ref[:, :width]).astype(BF16)
    loads[-1].wait()
    count = count_ref[0]
    first = iota((BLOCK, LANES), 1) < head_dim

    def both(pair):
        zero = jnp.zeros_like(pair)
        return jnp.concatenate([jnp.where(first, pair, zero), jnp.where(first, zero, pair)], axis=0)

    def own(out):
        return jnp.concatenate([out[:head_dim, :BLOCK], out[head_dim:, BLOCK:]], axis=0)

    def pair_step(pair, carry):
        lane = pl.multiple_of(pair * LANES, LANES)
        cols = pl.ds(lane, LANES)
        vcols = pl.ds(pl.multiple_of(width + pair * LANES, LANES), LANES)
        qm = both(q_ref[:, cols])
        dom = both(do_ref[:, cols])
        k = kv_ref[:, cols]
        v = kv_ref[:, vcols]
        s = nt(k, qm) * scale
        s = jnp.concatenate(
            [jnp.where(j < count, s[j * BLOCK:(j + 1) * BLOCK], FAR) for j in range(slots)], axis=0
        )
        e = jnp.exp(s - jnp.max(s, axis=0, keepdims=True))
        p = e / jnp.sum(e, axis=0, keepdims=True)
        pb = p.astype(BF16)
        dp = nt(v, dom)
        dots = jnp.sum(dp * p, axis=0, keepdims=True)
        ds = (p * (dp - dots) * scale).astype(BF16)
        attt_ref[cols, :] = own(tn(v, pb)).astype(BF16)
        dq_ref[:, cols] = jnp.transpose(own(tn(k, ds))).astype(BF16)
        dkv_ref[:, cols] = nn(ds, qm).astype(BF16)
        dkv_ref[:, vcols] = nn(pb, dom).astype(BF16)
        return carry

    lax.fori_loop(0, width // LANES, pair_step, 0, unroll=2)
    layer = (x_ref[pl.ds(0, BLOCK), :] + tn(attt_ref[...], wout_ref[...])).astype(BF16)
    layer_ref[...] = nn(to_order, layer).astype(BF16)
    att = nt(attt_ref[...], to_order).astype(BF16)
    lane_blocks = width // LANES
    gains = jnp.zeros((1, width), F32)
    dn_ref[...] = nt(dkv_ref[...], wqkv_ref[:, width:])
    for j in range(slots):
        rows = pl.ds(j * BLOCK, BLOCK)
        dn = dn_ref[rows, :]
        if j == 0:
            dn = dn + nt(dq_ref[...], wqkv_ref[:, :width])
        x = x_ref[rows, :]
        inv = inv_ref[rows, :][:, :1]
        gains = gains + jnp.sum(dn * (x * inv), axis=0, keepdims=True)
        scaled = dn * gain
        out = inv * scaled - x * (inv * inv * inv * jnp.mean(scaled * x, axis=1, keepdims=True))
        if j == 0:
            out = out + cots_ref[...].astype(F32)
        if fits:
            n_dev = ret_ref.shape[0]
            for lb in range(lane_blocks):
                piece = out[:, lb * LANES:(lb + 1) * LANES].reshape(n_dev, 8, LANES)
                ret_ref[:, pl.ds((j * lane_blocks + lb) * 8, 8), :] = piece.astype(BF16)
        else:
            ret_ref[j] = out.astype(BF16)
    if not fits:
        gain_out_ref[...] = gains
        att_out_ref[...] = att
        return
    base = slots * lane_blocks * 8
    feats = width // n_dev
    ret_ref[:, pl.ds(base, feats), :] = att.reshape(n_dev, feats, LANES)
    high = gains.astype(BF16).astype(F32)
    low = gains - high
    row = iota((8, LANES), 0)
    for part, value in enumerate((high, low)):
        tile = jnp.zeros((8, LANES), F32)
        for lb in range(lane_blocks):
            tile = jnp.where(row == lb, value[:, lb * LANES:(lb + 1) * LANES], tile)
        tile = jnp.broadcast_to(tile.astype(BF16)[None], (n_dev, 8, LANES))
        ret_ref[:, pl.ds(base + feats + part * 8, 8), :] = tile


def finish_kernel(
    n_dev, slots, masks, norm_scale, place_ref, table_ref, back_ref, one_ref, *rest
):
    sources = rest[:len(masks)]
    out_ref, gw_ref, gain_ref, acc_ref, sems = rest[len(masks):len(masks) + 5]
    cots = rest[len(masks) + 5:]
    loads = [
        pltpu.make_async_copy(source, target, sems.at[at])
        for at, (source, target) in enumerate(zip(sources, cots))
    ]
    for load in loads:
        load.start()
    rows, width = out_ref.shape
    lane_blocks = width // LANES
    size = lane_blocks * 8
    acc_ref[...] = jnp.zeros_like(acc_ref)

    def add(dest, carry):
        for slot in range(slots):
            block = table_ref[dest, 0, rows + slot]
            acc_ref[block] += back_ref[dest, pl.ds(slot * size, size), :].astype(F32)
        return carry

    lax.fori_loop(0, n_dev, add, 0, unroll=2)
    upper, seat = place_ref[0], place_ref[1]
    me = upper * (n_dev // 2) + seat
    one = one_ref[upper]
    for lb in range(lane_blocks):
        total = acc_ref[:, pl.ds(lb * 8, 8), :].reshape(rows, LANES).astype(BF16)
        out_ref[:, pl.ds(lb * LANES, LANES)] = nn(one, total).astype(BF16)
    base = slots * size
    feats = width // n_dev
    acc = jnp.zeros((feats, width), F32)
    for group, ref, load in zip(masks, cots, loads):
        load.wait()
        for at, mask in enumerate(group):
            att = back_ref[me ^ mask, pl.ds(base, feats), :]
            acc = acc + nn(att, ref[pl.ds(at * rows, rows), :])
    gw_ref[...] = acc * norm_scale
    tile = jnp.zeros((8, LANES), F32)
    for dest in range(n_dev):
        for part in range(2):
            tile = tile + back_ref[dest, pl.ds(base + feats + part * 8, 8), :].astype(F32)
    gain_ref[...] = tile * norm_scale


VM = pl.BlockSpec(memory_space=pltpu.VMEM)
SM = pl.BlockSpec(memory_space=pltpu.SMEM)
HB = pl.BlockSpec(memory_space=pltpu.HBM)


def near_core(x):
    return pltpu.with_memory_space_constraint(x, pltpu.VMEM)


def swap(block, mask):
    n_dev = lax.axis_size("ctx")
    return lax.ppermute(block, "ctx", [(i, i ^ mask) for i in range(n_dev)])


def per_device(
    raster_tokens, hilbert_perm, neighbors, neighbor_counts, norm_gain, w_qkv, w_out, cotangent
):
    n_dev = lax.axis_size("ctx")
    half = n_dev // 2
    me = lax.axis_index("ctx")
    rows, width = raster_tokens.shape
    slots = neighbors.shape[1]
    per_peer = rows // n_dev
    norm_scale = (rows * n_dev) ** (-0.5)
    n_rows = slots * BLOCK
    fits = per_peer % 8 == 0
    lane_blocks = width // LANES
    feats = width // n_dev
    place = jnp.stack([me // half, me % half]).astype(jnp.int32)
    note = jnp.concatenate([hilbert_perm, jnp.pad(neighbors[0], (0, rows - slots))])
    note = jnp.broadcast_to(note[None, None], (n_dev, 1, 2 * rows))
    mirror = swap(raster_tokens, half)
    other = swap(cotangent, half // 2)
    note = lax.all_to_all(note, "ctx", 0, 0, tiled=True)
    msg_shape = (half, 2, slots, per_peer, width) if fits else (8, LANES)
    sort_shape = (2, n_dev, per_peer, width) if fits else (2, rows, width)
    msg, one, in_order = pl.pallas_call(
        functools.partial(pack_kernel, n_dev, slots, per_peer),
        out_shape=(
            jax.ShapeDtypeStruct(msg_shape, BF16),
            jax.ShapeDtypeStruct((2, rows, rows), BF16),
            jax.ShapeDtypeStruct(sort_shape, BF16),
        ),
        in_specs=[SM, SM] + [VM] * 3,
        out_specs=(VM,) * 3,
    )(place, note, near_core(note), raster_tokens, near_core(mirror))
    table = note[:, 0, rows:rows + slots]
    if not fits:
        mine = lax.dynamic_slice_in_dim(table, place[0] * half, half, 0)
        msg = in_order.reshape(2, n_dev, per_peer, width)[:, mine].transpose(1, 0, 2, 3, 4)
    halves = [list(range(half)), list(range(half, n_dev))]
    arrived = lax.all_to_all(msg, "ctx", 0, 0, tiled=True, axis_index_groups=halves)
    held, cots, d_att, order = pl.pallas_call(
        ready_kernel,
        out_shape=(
            jax.ShapeDtypeStruct((2 * rows, width), BF16),
            jax.ShapeDtypeStruct((rows, width), BF16),
            jax.ShapeDtypeStruct((rows, width), BF16),
            jax.ShapeDtypeStruct((rows, rows), BF16),
        ),
        in_specs=[VM] * 4,
        out_specs=(VM,) * 4,
    )(cotangent, near_core(other), hilbert_perm[None], w_out)
    arrived, held = lax.optimization_barrier((arrived, held))
    names = [0, half // 2]
    bits = [1 << b for b in range(n_dev.bit_length() - 1)]
    for mask in [m for m in bits if m not in (1, 2, half, half // 2)]:
        held = jnp.concatenate([held, swap(held, mask)])
        names = names + [m ^ mask for m in names]
    across = swap(held, half)
    beside = swap(held, 2)
    if fits:
        ret_shape = (n_dev, slots * lane_blocks * 8 + feats + 16, LANES)
        extra_shapes = ()
    else:
        arrived = arrived.transpose(2, 1, 0, 3, 4).reshape(slots, rows, width)
        ret_shape = (slots, rows, width)
        extra_shapes = (
            jax.ShapeDtypeStruct((1, width), F32),
            jax.ShapeDtypeStruct((width, rows), BF16),
        )

    layer_out, ret, *extra = pl.pallas_call(
        functools.partial(main_kernel, fits),
        out_shape=(
            jax.ShapeDtypeStruct((rows, width), BF16),
            jax.ShapeDtypeStruct(ret_shape, BF16),
        ) + extra_shapes,
        in_specs=[SM] + [VM] * 5 + [HB] * 2,
        out_specs=(VM,) * (2 + len(extra_shapes)),
        scratch_shapes=[
            pltpu.VMEM((n_rows, width), F32),
            pltpu.VMEM((n_rows, LANES), F32),
            pltpu.VMEM((n_rows, width), BF16),
            pltpu.VMEM((rows, width), BF16),
            pltpu.VMEM((n_rows, 2 * width), BF16),
            pltpu.VMEM((width, rows), BF16),
            pltpu.VMEM((rows, width), BF16),
            pltpu.VMEM((n_rows, 2 * width), BF16),
            pltpu.VMEM((n_rows, width), F32),
            pltpu.VMEM(w_qkv.shape, BF16),
            pltpu.VMEM(w_out.shape, BF16),
            pltpu.SemaphoreType.DMA((4,)),
        ],
        cost_estimate=pl.CostEstimate(
            flops=14 * n_rows * width * width, bytes_accessed=16 * width * width, transcendentals=0
        ),
    )(
        neighbor_counts, near_core(arrived), order, norm_gain[None], cots, d_att, w_qkv, w_out,
    )

    if fits:
        back = lax.all_to_all(ret, "ctx", 0, 0, tiled=True)
    corner = swap(across, 2)
    pieces = [
        (names, held),
        ([m ^ half for m in names], across),
        ([m ^ 2 for m in names], beside),
        ([m ^ 2 ^ half for m in names], corner),
    ]
    for group, piece in list(pieces):
        pieces.append(([m ^ 1 for m in group], swap(piece, 1)))
    if fits:
        masks = [group for group, piece in pieces]
        grad_tokens, grad_w_out, grad_gain = pl.pallas_call(
            functools.partial(finish_kernel, n_dev, slots, masks, norm_scale),
            out_shape=(
                jax.ShapeDtypeStruct((rows, width), BF16),
                jax.ShapeDtypeStruct((feats, width), F32),
                jax.ShapeDtypeStruct((lane_blocks, LANES), F32),
            ),
            in_specs=[SM, SM, VM, VM] + [HB] * len(pieces),
            out_specs=(VM, VM, VM),
            scratch_shapes=[
                pltpu.VMEM((n_dev, lane_blocks * 8, LANES), F32),
                pltpu.SemaphoreType.DMA((len(pieces),)),
            ] + [pltpu.VMEM(piece.shape, BF16) for group, piece in pieces],
        )(place, note, near_core(back), one, *[piece for group, piece in pieces])
        return (layer_out, grad_tokens, grad_w_out, grad_gain.reshape(width))
    gains, att = extra
    high = gains.astype(BF16)
    low = (gains - high.astype(F32)).astype(BF16)
    ret = ret.reshape(slots, n_dev, per_peer, width).transpose(1, 0, 2, 3).reshape(n_dev, -1)
    both = jnp.broadcast_to(jnp.concatenate([high, low]).reshape(1, -1), (n_dev, 2 * width))
    sizes = (ret.shape[1], feats * rows)
    ret = jnp.concatenate([ret, att.reshape(n_dev, -1), both], axis=1).reshape(n_dev, -1, LANES)
    back = lax.all_to_all(ret, "ctx", 0, 0, tiled=True).reshape(n_dev, -1)
    rest = back[:, :sizes[0]].reshape(n_dev * slots, per_peer, width).astype(F32)
    total = jnp.zeros((n_dev, per_peer, width), F32).at[table.reshape(-1)].add(rest)
    grad_tokens = nn(one[place[0]], total.reshape(rows, width).astype(BF16)).astype(BF16)
    att = back[:, sizes[0]:sizes[0] + sizes[1]].reshape(n_dev, feats, rows)
    order = me ^ jnp.array(sum([group for group, piece in pieces], []))
    cots = jnp.concatenate([piece for group, piece in pieces]).reshape(n_dev, rows, width)
    grad_w_out = jnp.einsum("sft,stw->fw", att[order], cots, preferred_element_type=F32) * norm_scale
    parts = back[:, sizes[0] + sizes[1]:].reshape(n_dev, 2, width).astype(F32)
    grad_gain = jnp.sum(parts, axis=(0, 1)) * norm_scale
    return (layer_out, grad_tokens, grad_w_out, grad_gain)


def solution(mesh):
    placed = (
        P(("groups", "ctx"), None),
        P(("groups", "ctx")),
        P(("groups", "ctx"), None),
        P(("groups", "ctx")),
        P(),
        P(),
        P(),
        P(("groups", "ctx"), None),
    )

    return jax.shard_map(
        per_device,
        mesh=mesh,
        in_specs=placed,
        out_specs=(
            P(("groups", "ctx"), None),
            P(("groups", "ctx"), None),
            P(("groups", "ctx"), None),
            P("groups"),
        ),
        check_vma=False,
    )
```

```python
import functools
import math

import jax
import jax.numpy as jnp
from jax import lax
from jax.experimental import pallas as pl
from jax.experimental.pallas import tpu as pltpu
from jax.sharding import PartitionSpec as P


HEADS = 16
BLOCK = 128
LANES = 128
EPS = 1e-06
FAR = -1e30
F32 = jnp.float32
BF16 = jnp.bfloat16


def iota(shape, dim):
    return lax.broadcasted_iota(jnp.int32, shape, dim)


def nn(a, b):
    return jnp.dot(a, b, preferred_element_type=F32)


def nt(a, b):
    return lax.dot_general(a, b, (((1,), (1,)), ((), ())), preferred_element_type=F32)


def tn(a, b):
    return lax.dot_general(a, b, (((0,), (0,)), ((), ())), preferred_element_type=F32)


def ranks(key_col, key_row, dim):
    if dim == 0:
        return jnp.sum((key_col < key_row).astype(F32), axis=0, keepdims=True).astype(jnp.int32)
    return jnp.sum((key_row < key_col).astype(F32), axis=1, keepdims=True).astype(jnp.int32)


def column_of(row):
    n = row.shape[1]
    wide = jnp.broadcast_to(row.astype(F32), (n, n))
    return jnp.transpose(wide)[:, :1].astype(jnp.int32)


def row_of(col):
    n = col.shape[0]
    wide = jnp.broadcast_to(col.astype(F32), (n, n))
    return jnp.transpose(wide)[:1, :].astype(jnp.int32)


def pack_kernel(n_dev, slots, per_peer, place_ref, table_ref, note_ref, own_ref, mirror_ref, msg_ref, one_ref, sorted_ref):
    rows, width = own_ref.shape
    half = n_dev // 2
    upper, seat = place_ref[0], place_ref[1]
    for part in range(2):
        target = (part * half + seat) * rows + iota((rows, 1), 0)

        def hit(block, acc):
            line = note_ref[block][:, :rows]
            return acc + jnp.where(line == target, block, 0)

        found = lax.fori_loop(0, n_dev, hit, jnp.zeros((rows, rows), jnp.int32), unroll=4)
        home = jnp.sum(found.astype(F32), axis=1, keepdims=True).astype(jnp.int32)
        key_col = home * rows + iota((rows, 1), 0)
        key_row = row_of(key_col)
        slot_row = ranks(key_col, key_row, 0)
        slot_col = ranks(key_col, key_row, 1)
        pick = (slot_row == iota((rows, rows), 0)).astype(BF16)
        one_ref[part] = (slot_col == iota((rows, rows), 1)).astype(BF16)
        chunk = jnp.where(upper == part, own_ref[...], mirror_ref[...])
        ordered = nn(pick, chunk)
        if per_peer % 8 == 0:
            sorted_ref[part] = ordered.reshape(n_dev, per_peer, width).astype(BF16)
        else:
            sorted_ref[part] = ordered.astype(BF16)
    if per_peer % 8 == 0:

        def place(dest, carry):
            for slot in range(slots):
                block = table_ref[upper * half + dest, 0, rows + slot]
                for part in range(2):
                    msg_ref[dest, part, slot] = sorted_ref[part, block]
            return carry

        lax.fori_loop(0, half, place, 0, unroll=2)


def ready_kernel(
    cot_ref, other_ref, perm_ref, wout_ref, held_ref, cots_ref, do_ref, order_ref
):
    rows = cot_ref.shape[0]
    held_ref[pl.ds(0, rows), :] = cot_ref[...]
    held_ref[pl.ds(rows, rows), :] = other_ref[...]
    key_row = perm_ref[...]
    key_col = column_of(key_row)
    slot_row = ranks(key_col, key_row, 0)
    slot_col = ranks(key_col, key_row, 1)
    to_arrival = (slot_row == iota((BLOCK, BLOCK), 0)).astype(BF16)
    order_ref[...] = (slot_col == iota((BLOCK, BLOCK), 1)).astype(BF16)
    cots_ref[...] = nn(to_arrival, cot_ref[...]).astype(BF16)
    do_ref[...] = nt(cots_ref[...], wout_ref[...]).astype(BF16)


def main_kernel(
    fits, count_ref, arrived_ref, order_ref, gain_ref, cots_ref, do_ref, wqkv_hbm, wout_hbm,
    layer_ref, ret_ref, *rest
):
    if fits:
        x_ref, inv_ref, nrm_ref, q_ref, kv_ref, attt_ref, dq_ref, dkv_ref, dn_ref, wqkv_ref, wout_ref, sems, ret_v = rest
    else:
        gain_out_ref, att_out_ref, x_ref, inv_ref, nrm_ref, q_ref, kv_ref, attt_ref, dq_ref, dkv_ref, dn_ref, wqkv_ref, wout_ref, sems, ret_v = rest
    n_rows, width = x_ref.shape
    slots = n_rows // BLOCK
    head_dim = width // HEADS
    gain = gain_ref[...]
    to_order = order_ref[...]
    loads = []
    for at, (start, size) in enumerate(((width, width), (2 * width, width), (0, width))):
        part = pl.ds(start, size)
        loads.append(pltpu.make_async_copy(wqkv_hbm.at[:, part], wqkv_ref.at[:, part], sems.at[at]))
    loads.append(pltpu.make_async_copy(wout_hbm, wout_ref, sems.at[3]))
    for load in loads:
        load.start()
    for j in range(slots):
        if fits:
            part_rows = BLOCK // 2
            for part in range(2):
                x = arrived_ref[:, part, j].astype(F32).reshape(part_rows, width)
                x_ref[pl.ds(j * BLOCK + part * part_rows, part_rows), :] = x
        else:
            x_ref[pl.ds(j * BLOCK, BLOCK), :] = arrived_ref[j].astype(F32)
        x = x_ref[pl.ds(j * BLOCK, BLOCK), :]
        inv = lax.rsqrt(jnp.mean(x * x, axis=1, keepdims=True) + EPS)
        inv_ref[pl.ds(j * BLOCK, BLOCK), :] = jnp.broadcast_to(inv, (BLOCK, LANES))
        nrm_ref[pl.ds(j * BLOCK, BLOCK), :] = (x * inv * gain).astype(BF16)
    scale = head_dim ** (-0.5)
    assert math.frexp(scale)[0] == 0.5
    for at in range(2):
        loads[at].wait()
        weight = wqkv_ref[:, (at + 1) * width:(at + 2) * width]
        kv_ref[:, pl.ds(at * width, width)] = nn(nrm_ref[...], weight).astype(BF16)
    loads[2].wait()
    q_ref[...] = nn(nrm_ref[pl.ds(0, BLOCK), :], wqkv_ref[:, :width]).astype(BF16)
    count = count_ref[0]
    first = iota((BLOCK, LANES), 1) < head_dim

    def both(pair):
        zero = jnp.zeros_like(pair)
        return jnp.concatenate([jnp.where(first, pair, zero), jnp.where(first, zero, pair)], axis=0)

    def own(out):
        return jnp.concatenate([out[:head_dim, :BLOCK], out[head_dim:, BLOCK:]], axis=0)

    def pair_step(pair, carry):
        lane = pl.multiple_of(pair * LANES, LANES)
        cols = pl.ds(lane, LANES)
        vcols = pl.ds(pl.multiple_of(width + pair * LANES, LANES), LANES)
        qm = both(q_ref[:, cols])
        dom = both(do_ref[:, cols])
        k = kv_ref[:, cols]
        v = kv_ref[:, vcols]
        qs = qm * jnp.asarray(scale, BF16)
        s = nt(k, qs)
        s = jnp.concatenate(
            [jnp.where(j < count, s[j * BLOCK:(j + 1) * BLOCK], FAR) for j in range(slots)], axis=0
        )
        e = jnp.exp(s - jnp.max(s, axis=0, keepdims=True))
        p = e * (1.0 / jnp.sum(e, axis=0, keepdims=True))
        pb = p.astype(BF16)
        dp = nt(v, dom)
        dots = jnp.sum(dp * p, axis=0, keepdims=True)
        ds = (p * (dp - dots)).astype(BF16)
        attt_ref[cols, :] = own(tn(v, pb)).astype(BF16)
        dq_ref[:, cols] = jnp.transpose(own(tn(k, ds)) * scale).astype(BF16)
        dkv_ref[:, cols] = nn(ds, qs).astype(BF16)
        dkv_ref[:, vcols] = nn(pb, dom).astype(BF16)
        return carry

    lax.fori_loop(0, width // LANES, pair_step, 0, unroll=8)
    loads[3].wait()
    layer = (x_ref[pl.ds(0, BLOCK), :] + tn(attt_ref[...], wout_ref[...])).astype(BF16)
    layer_ref[...] = nn(to_order, layer).astype(BF16)
    att = nt(attt_ref[...], to_order).astype(BF16)
    lane_blocks = width // LANES
    gains = jnp.zeros((1, width), F32)
    stores = []
    dn_ref[...] = nt(dkv_ref[...], wqkv_ref[:, width:])
    for j in range(slots):
        rows = pl.ds(j * BLOCK, BLOCK)
        dn = dn_ref[rows, :]
        if j == 0:
            dn = dn + nt(dq_ref[...], wqkv_ref[:, :width])
        x = x_ref[rows, :]
        inv = inv_ref[rows, :][:, :1]
        gains = gains + jnp.sum(dn * (x * inv), axis=0, keepdims=True)
        scaled = dn * gain
        out = inv * scaled - x * (inv * inv * inv * jnp.mean(scaled * x, axis=1, keepdims=True))
        if j == 0:
            out = out + cots_ref[...].astype(F32)
        if fits:
            n_dev = ret_ref.shape[0]
            for lb in range(lane_blocks):
                piece = out[:, lb * LANES:(lb + 1) * LANES].reshape(n_dev, 8, LANES)
                ret_v[:, pl.ds((j * lane_blocks + lb) * 8, 8), :] = piece.astype(BF16)
            region = pl.ds(j * lane_blocks * 8, lane_blocks * 8)
            stores.append(pltpu.make_async_copy(ret_v.at[:, region], ret_ref.at[:, region], sems.at[4 + j]))
            stores[-1].start()
        else:
            ret_ref[j] = out.astype(BF16)
    if not fits:
        gain_out_ref[...] = gains
        att_out_ref[...] = att
        return
    base = slots * lane_blocks * 8
    feats = width // n_dev
    ret_v[:, pl.ds(base, feats), :] = att.reshape(n_dev, feats, LANES)
    high = gains.astype(BF16).astype(F32)
    low = gains - high
    row = iota((8, LANES), 0)
    for part, value in enumerate((high, low)):
        tile = jnp.zeros((8, LANES), F32)
        for lb in range(lane_blocks):
            tile = jnp.where(row == lb, value[:, lb * LANES:(lb + 1) * LANES], tile)
        tile = jnp.broadcast_to(tile.astype(BF16)[None], (n_dev, 8, LANES))
        ret_v[:, pl.ds(base + feats + part * 8, 8), :] = tile
    region = pl.ds(base, feats + 16)
    stores.append(pltpu.make_async_copy(ret_v.at[:, region], ret_ref.at[:, region], sems.at[4 + slots]))
    stores[-1].start()
    for store in stores:
        store.wait()


def finish_kernel(
    n_dev, slots, masks, norm_scale, place_ref, table_ref, back_ref, one_ref, *rest
):
    sources = rest[:len(masks)]
    out_ref, gw_ref, gain_ref, acc_ref, sems = rest[len(masks):len(masks) + 5]
    cots = rest[len(masks) + 5:]
    loads = [
        pltpu.make_async_copy(source, target, sems.at[at])
        for at, (source, target) in enumerate(zip(sources, cots))
    ]
    for load in loads:
        load.start()
    rows, width = out_ref.shape
    lane_blocks = width // LANES
    size = lane_blocks * 8
    acc_ref[...] = jnp.zeros_like(acc_ref)

    def add(dest, carry):
        for slot in range(slots):
            block = table_ref[dest, 0, rows + slot]
            acc_ref[block] += back_ref[dest, pl.ds(slot * size, size), :].astype(F32)
        return carry

    lax.fori_loop(0, n_dev, add, 0, unroll=2)
    upper, seat = place_ref[0], place_ref[1]
    me = upper * (n_dev // 2) + seat
    one = one_ref[upper]
    for lb in range(lane_blocks):
        total = acc_ref[:, pl.ds(lb * 8, 8), :].reshape(rows, LANES).astype(BF16)
        out_ref[:, pl.ds(lb * LANES, LANES)] = nn(one, total).astype(BF16)
    base = slots * size
    feats = width // n_dev
    acc = jnp.zeros((feats, width), F32)
    for group, ref, load in zip(masks, cots, loads):
        load.wait()
        att = jnp.concatenate([back_ref[me ^ mask, pl.ds(base, feats), :] for mask in group], axis=1)
        acc = acc + nn(att, ref[...])
    gw_ref[...] = acc * norm_scale
    tile = jnp.zeros((8, LANES), F32)
    for dest in range(n_dev):
        for part in range(2):
            tile = tile + back_ref[dest, pl.ds(base + feats + part * 8, 8), :].astype(F32)
    gain_ref[...] = tile * norm_scale


VM = pl.BlockSpec(memory_space=pltpu.VMEM)
SM = pl.BlockSpec(memory_space=pltpu.SMEM)
HB = pl.BlockSpec(memory_space=pltpu.HBM)


def near_core(x):
    return pltpu.with_memory_space_constraint(x, pltpu.VMEM)


def swap(block, mask):
    n_dev = lax.axis_size("ctx")
    return lax.ppermute(block, "ctx", [(i, i ^ mask) for i in range(n_dev)])


def per_device(
    raster_tokens, hilbert_perm, neighbors, neighbor_counts, norm_gain, w_qkv, w_out, cotangent
):
    n_dev = lax.axis_size("ctx")
    half = n_dev // 2
    me = lax.axis_index("ctx")
    rows, width = raster_tokens.shape
    slots = neighbors.shape[1]
    per_peer = rows // n_dev
    norm_scale = (rows * n_dev) ** (-0.5)
    n_rows = slots * BLOCK
    fits = per_peer % 8 == 0
    lane_blocks = width // LANES
    feats = width // n_dev
    place = jnp.stack([me // half, me % half]).astype(jnp.int32)
    note = jnp.concatenate([hilbert_perm, jnp.pad(neighbors[0], (0, rows - slots))])
    note = jnp.broadcast_to(note[None, None], (n_dev, 1, 2 * rows))
    mirror = swap(raster_tokens, half)
    other = swap(cotangent, half // 2)
    note = lax.all_to_all(note, "ctx", 0, 0, tiled=True)
    msg_shape = (half, 2, slots, per_peer, width) if fits else (8, LANES)
    sort_shape = (2, n_dev, per_peer, width) if fits else (2, rows, width)
    msg, one, *in_order = pl.pallas_call(
        functools.partial(pack_kernel, n_dev, slots, per_peer),
        out_shape=(
            jax.ShapeDtypeStruct(msg_shape, BF16),
            jax.ShapeDtypeStruct((2, rows, rows), BF16),
        ) + (() if fits else (jax.ShapeDtypeStruct(sort_shape, BF16),)),
        in_specs=[SM, SM] + [VM] * 3,
        out_specs=(VM,) * (2 if fits else 3),
        scratch_shapes=[pltpu.VMEM(sort_shape, BF16)] if fits else [],
    )(place, note, near_core(note), raster_tokens, near_core(mirror))
    table = note[:, 0, rows:rows + slots]
    if not fits:
        mine = lax.dynamic_slice_in_dim(table, place[0] * half, half, 0)
        msg = in_order[0].reshape(2, n_dev, per_peer, width)[:, mine].transpose(1, 0, 2, 3, 4)
    halves = [list(range(half)), list(range(half, n_dev))]
    arrived = lax.all_to_all(msg, "ctx", 0, 0, tiled=True, axis_index_groups=halves)
    held, cots, d_att, order = pl.pallas_call(
        ready_kernel,
        out_shape=(
            jax.ShapeDtypeStruct((2 * rows, width), BF16),
            jax.ShapeDtypeStruct((rows, width), BF16),
            jax.ShapeDtypeStruct((rows, width), BF16),
            jax.ShapeDtypeStruct((rows, rows), BF16),
        ),
        in_specs=[VM] * 4,
        out_specs=(VM,) * 4,
    )(cotangent, near_core(other), hilbert_perm[None], w_out)
    arrived, held = lax.optimization_barrier((arrived, held))
    names = [0, half // 2]
    bits = [1 << b for b in range(n_dev.bit_length() - 1)]
    for mask in [m for m in bits if m not in (1, 2, half, half // 2)]:
        held = jnp.concatenate([held, swap(held, mask)])
        names = names + [m ^ mask for m in names]
    across = swap(held, half)
    beside = swap(held, 2)
    if fits:
        ret_shape = (n_dev, slots * lane_blocks * 8 + feats + 16, LANES)
        extra_shapes = ()
    else:
        arrived = arrived.transpose(2, 1, 0, 3, 4).reshape(slots, rows, width)
        ret_shape = (slots, rows, width)
        extra_shapes = (
            jax.ShapeDtypeStruct((1, width), F32),
            jax.ShapeDtypeStruct((width, rows), BF16),
        )

    layer_out, ret, *extra = pl.pallas_call(
        functools.partial(main_kernel, fits),
        out_shape=(
            jax.ShapeDtypeStruct((rows, width), BF16),
            jax.ShapeDtypeStruct(ret_shape, BF16),
        ) + extra_shapes,
        in_specs=[SM] + [VM] * 5 + [HB] * 2,
        out_specs=(VM, HB if fits else VM) + (VM,) * len(extra_shapes),
        scratch_shapes=[
            pltpu.VMEM((n_rows, width), F32),
            pltpu.VMEM((n_rows, LANES), F32),
            pltpu.VMEM((n_rows, width), BF16),
            pltpu.VMEM((rows, width), BF16),
            pltpu.VMEM((n_rows, 2 * width), BF16),
            pltpu.VMEM((width, rows), BF16),
            pltpu.VMEM((rows, width), BF16),
            pltpu.VMEM((n_rows, 2 * width), BF16),
            pltpu.VMEM((n_rows, width), F32),
            pltpu.VMEM(w_qkv.shape, BF16),
            pltpu.VMEM(w_out.shape, BF16),
            pltpu.SemaphoreType.DMA((5 + slots,)),
            pltpu.VMEM(ret_shape if fits else (8, LANES), BF16),
        ],
        cost_estimate=pl.CostEstimate(
            flops=14 * n_rows * width * width, bytes_accessed=16 * width * width, transcendentals=0
        ),
    )(
        neighbor_counts, near_core(arrived), order, norm_gain[None], cots, d_att, w_qkv, w_out,
    )

    if fits:
        back = lax.all_to_all(ret, "ctx", 0, 0, tiled=True)
    corner = swap(across, 2)
    pieces = [
        (names, held),
        ([m ^ half for m in names], across),
        ([m ^ 2 for m in names], beside),
        ([m ^ 2 ^ half for m in names], corner),
    ]
    for group, piece in list(pieces):
        pieces.append(([m ^ 1 for m in group], swap(piece, 1)))
    if fits:
        masks = [group for group, piece in pieces]
        grad_tokens, grad_w_out, grad_gain = pl.pallas_call(
            functools.partial(finish_kernel, n_dev, slots, masks, norm_scale),
            out_shape=(
                jax.ShapeDtypeStruct((rows, width), BF16),
                jax.ShapeDtypeStruct((feats, width), F32),
                jax.ShapeDtypeStruct((lane_blocks, LANES), F32),
            ),
            in_specs=[SM, SM, VM, VM] + [HB] * len(pieces),
            out_specs=(VM, VM, VM),
            scratch_shapes=[
                pltpu.VMEM((n_dev, lane_blocks * 8, LANES), F32),
                pltpu.SemaphoreType.DMA((len(pieces),)),
            ] + [pltpu.VMEM(piece.shape, BF16) for group, piece in pieces],
        )(place, note, near_core(back), one, *[piece for group, piece in pieces])
        return (layer_out, grad_tokens, grad_w_out, grad_gain.reshape(width))
    gains, att = extra
    high = gains.astype(BF16)
    low = (gains - high.astype(F32)).astype(BF16)
    ret = ret.reshape(slots, n_dev, per_peer, width).transpose(1, 0, 2, 3).reshape(n_dev, -1)
    both = jnp.broadcast_to(jnp.concatenate([high, low]).reshape(1, -1), (n_dev, 2 * width))
    sizes = (ret.shape[1], feats * rows)
    ret = jnp.concatenate([ret, att.reshape(n_dev, -1), both], axis=1).reshape(n_dev, -1, LANES)
    back = lax.all_to_all(ret, "ctx", 0, 0, tiled=True).reshape(n_dev, -1)
    rest = back[:, :sizes[0]].reshape(n_dev * slots, per_peer, width).astype(F32)
    total = jnp.zeros((n_dev, per_peer, width), F32).at[table.reshape(-1)].add(rest)
    grad_tokens = nn(one[place[0]], total.reshape(rows, width).astype(BF16)).astype(BF16)
    att = back[:, sizes[0]:sizes[0] + sizes[1]].reshape(n_dev, feats, rows)
    order = me ^ jnp.array(sum([group for group, piece in pieces], []))
    cots = jnp.concatenate([piece for group, piece in pieces]).reshape(n_dev, rows, width)
    grad_w_out = jnp.einsum("sft,stw->fw", att[order], cots, preferred_element_type=F32) * norm_scale
    parts = back[:, sizes[0] + sizes[1]:].reshape(n_dev, 2, width).astype(F32)
    grad_gain = jnp.sum(parts, axis=(0, 1)) * norm_scale
    return (layer_out, grad_tokens, grad_w_out, grad_gain)


def solution(mesh):
    placed = (
        P(("groups", "ctx"), None),
        P(("groups", "ctx")),
        P(("groups", "ctx"), None),
        P(("groups", "ctx")),
        P(),
        P(),
        P(),
        P(("groups", "ctx"), None),
    )

    return jax.shard_map(
        per_device,
        mesh=mesh,
        in_specs=placed,
        out_specs=(
            P(("groups", "ctx"), None),
            P(("groups", "ctx"), None),
            P(("groups", "ctx"), None),
            P("groups"),
        ),
        check_vma=False,
    )
```

```python
import functools
import math

import jax
import jax.numpy as jnp
from jax import lax
from jax.experimental import pallas as pl
from jax.experimental.pallas import tpu as pltpu
from jax.sharding import PartitionSpec as P


HEADS = 16
BLOCK = 128
LANES = 128
EPS = 1e-06
FAR = -1e30
F32 = jnp.float32
BF16 = jnp.bfloat16


def iota(shape, dim):
    return lax.broadcasted_iota(jnp.int32, shape, dim)


def nn(a, b):
    return jnp.dot(a, b, preferred_element_type=F32)


def nt(a, b):
    return lax.dot_general(a, b, (((1,), (1,)), ((), ())), preferred_element_type=F32)


def tn(a, b):
    return lax.dot_general(a, b, (((0,), (0,)), ((), ())), preferred_element_type=F32)


def ranks(key_col, key_row, dim):
    if dim == 0:
        return jnp.sum((key_col < key_row).astype(F32), axis=0, keepdims=True).astype(jnp.int32)
    return jnp.sum((key_row < key_col).astype(F32), axis=1, keepdims=True).astype(jnp.int32)


def column_of(row):
    n = row.shape[1]
    wide = jnp.broadcast_to(row.astype(F32), (n, n))
    return jnp.transpose(wide)[:, :1].astype(jnp.int32)


def row_of(col):
    n = col.shape[0]
    wide = jnp.broadcast_to(col.astype(F32), (n, n))
    return jnp.transpose(wide)[:1, :].astype(jnp.int32)


def note_kernel(list_ref, perm_ref, out_ref):
    n_dev, rows = out_ref.shape[0], perm_ref.shape[1]
    lane = iota((1, rows), 1)
    listed = jnp.zeros((1, rows), jnp.int32)
    for slot in range(list_ref.shape[1]):
        listed = jnp.where(lane == slot, list_ref[0, slot], listed)
    both = jnp.concatenate([perm_ref[...], listed], axis=1)
    out_ref[...] = jnp.broadcast_to(both[None], (n_dev, 1, 2 * rows))


def pack_kernel(n_dev, slots, per_peer, place_ref, table_ref, note_ref, own_ref, mirror_ref, msg_ref, one_ref, sorted_ref):
    rows, width = own_ref.shape
    half = n_dev // 2
    upper, seat = place_ref[0], place_ref[1]
    for part in range(2):
        target = (part * half + seat) * rows + iota((rows, 1), 0)

        def hit(block, acc):
            line = note_ref[block][:, :rows]
            return acc + jnp.where(line == target, block, 0)

        found = lax.fori_loop(0, n_dev, hit, jnp.zeros((rows, rows), jnp.int32), unroll=4)
        home = jnp.sum(found.astype(F32), axis=1, keepdims=True).astype(jnp.int32)
        key_col = home * rows + iota((rows, 1), 0)
        key_row = row_of(key_col)
        slot_row = ranks(key_col, key_row, 0)
        slot_col = ranks(key_col, key_row, 1)
        pick = (slot_row == iota((rows, rows), 0)).astype(BF16)
        one_ref[part] = (slot_col == iota((rows, rows), 1)).astype(BF16)
        chunk = jnp.where(upper == part, own_ref[...], mirror_ref[...])
        ordered = nn(pick, chunk)
        if per_peer % 8 == 0:
            sorted_ref[part] = ordered.reshape(n_dev, per_peer, width).astype(BF16)
        else:
            sorted_ref[part] = ordered.astype(BF16)
    if per_peer % 8 == 0:

        def place(dest, carry):
            for slot in range(slots):
                block = table_ref[upper * half + dest, 0, rows + slot]
                for part in range(2):
                    msg_ref[dest, part, slot] = sorted_ref[part, block]
            return carry

        lax.fori_loop(0, half, place, 0, unroll=2)


def ready_kernel(
    cot_ref, other_ref, perm_ref, wout_ref, held_ref, cots_ref, do_ref, order_ref
):
    rows = cot_ref.shape[0]
    held_ref[pl.ds(0, rows), :] = cot_ref[...]
    held_ref[pl.ds(rows, rows), :] = other_ref[...]
    key_row = perm_ref[...]
    key_col = column_of(key_row)
    slot_row = ranks(key_col, key_row, 0)
    slot_col = ranks(key_col, key_row, 1)
    to_arrival = (slot_row == iota((BLOCK, BLOCK), 0)).astype(BF16)
    order_ref[...] = (slot_col == iota((BLOCK, BLOCK), 1)).astype(BF16)
    cots_ref[...] = nn(to_arrival, cot_ref[...]).astype(BF16)
    do_ref[...] = nt(cots_ref[...], wout_ref[...]).astype(BF16)


def main_kernel(
    fits, count_ref, arrived_ref, order_ref, gain_ref, cots_ref, do_ref, wqkv_hbm, wout_hbm,
    layer_ref, ret_ref, *rest
):
    if fits:
        x_ref, inv_ref, nrm_ref, q_ref, kv_ref, attt_ref, dq_ref, dkv_ref, dn_ref, wqkv_ref, wout_ref, sems, ret_v = rest
    else:
        gain_out_ref, att_out_ref, x_ref, inv_ref, nrm_ref, q_ref, kv_ref, attt_ref, dq_ref, dkv_ref, dn_ref, wqkv_ref, wout_ref, sems, ret_v = rest
    n_rows, width = x_ref.shape
    slots = n_rows // BLOCK
    head_dim = width // HEADS
    gain = gain_ref[...]
    to_order = order_ref[...]
    loads = []
    for at, (start, size) in enumerate(((width, width), (2 * width, width), (0, width))):
        part = pl.ds(start, size)
        loads.append(pltpu.make_async_copy(wqkv_hbm.at[:, part], wqkv_ref.at[:, part], sems.at[at]))
    loads.append(pltpu.make_async_copy(wout_hbm, wout_ref, sems.at[3]))
    for load in loads:
        load.start()
    for j in range(slots):
        if fits:
            part_rows = BLOCK // 2
            for part in range(2):
                x = arrived_ref[:, part, j].astype(F32).reshape(part_rows, width)
                x_ref[pl.ds(j * BLOCK + part * part_rows, part_rows), :] = x
        else:
            x_ref[pl.ds(j * BLOCK, BLOCK), :] = arrived_ref[j].astype(F32)
        x = x_ref[pl.ds(j * BLOCK, BLOCK), :]
        inv = lax.rsqrt(jnp.mean(x * x, axis=1, keepdims=True) + EPS)
        inv_ref[pl.ds(j * BLOCK, BLOCK), :] = jnp.broadcast_to(inv, (BLOCK, LANES))
        nrm_ref[pl.ds(j * BLOCK, BLOCK), :] = (x * inv * gain).astype(BF16)
    scale = head_dim ** (-0.5)
    assert math.frexp(scale)[0] == 0.5
    for at in range(2):
        loads[at].wait()
        weight = wqkv_ref[:, (at + 1) * width:(at + 2) * width]
        kv_ref[:, pl.ds(at * width, width)] = nn(nrm_ref[...], weight).astype(BF16)
    loads[2].wait()
    q_ref[...] = nn(nrm_ref[pl.ds(0, BLOCK), :], wqkv_ref[:, :width]).astype(BF16)
    count = count_ref[0]
    first = iota((BLOCK, LANES), 1) < head_dim

    def both(pair):
        zero = jnp.zeros_like(pair)
        return jnp.concatenate([jnp.where(first, pair, zero), jnp.where(first, zero, pair)], axis=0)

    def own(out):
        return jnp.concatenate([out[:head_dim, :BLOCK], out[head_dim:, BLOCK:]], axis=0)

    def pair_step(pair, carry):
        lane = pl.multiple_of(pair * LANES, LANES)
        cols = pl.ds(lane, LANES)
        vcols = pl.ds(pl.multiple_of(width + pair * LANES, LANES), LANES)
        qm = both(q_ref[:, cols])
        dom = both(do_ref[:, cols])
        k = kv_ref[:, cols]
        v = kv_ref[:, vcols]
        qs = qm * jnp.asarray(scale, BF16)
        s = nt(k, qs)
        s = jnp.concatenate(
            [jnp.where(j < count, s[j * BLOCK:(j + 1) * BLOCK], FAR) for j in range(slots)], axis=0
        )
        e = jnp.exp(s - jnp.max(s, axis=0, keepdims=True))
        p = e * (1.0 / jnp.sum(e, axis=0, keepdims=True))
        pb = p.astype(BF16)
        dp = nt(v, dom)
        dots = jnp.sum(dp * p, axis=0, keepdims=True)
        ds = (p * (dp - dots)).astype(BF16)
        attt_ref[cols, :] = own(tn(v, pb)).astype(BF16)
        dq_ref[:, cols] = jnp.transpose(own(tn(k, ds)) * scale).astype(BF16)
        dkv_ref[:, cols] = nn(ds, qs).astype(BF16)
        dkv_ref[:, vcols] = nn(pb, dom).astype(BF16)
        return carry

    lax.fori_loop(0, width // LANES, pair_step, 0, unroll=8)
    loads[3].wait()
    layer = (x_ref[pl.ds(0, BLOCK), :] + tn(attt_ref[...], wout_ref[...])).astype(BF16)
    layer_ref[...] = nn(to_order, layer).astype(BF16)
    att = nt(attt_ref[...], to_order).astype(BF16)
    lane_blocks = width // LANES
    gains = jnp.zeros((1, width), F32)
    stores = []
    dn_ref[...] = nt(dkv_ref[...], wqkv_ref[:, width:])
    for j in range(slots):
        rows = pl.ds(j * BLOCK, BLOCK)
        dn = dn_ref[rows, :]
        if j == 0:
            dn = dn + nt(dq_ref[...], wqkv_ref[:, :width])
        x = x_ref[rows, :]
        inv = inv_ref[rows, :][:, :1]
        gains = gains + jnp.sum(dn * (x * inv), axis=0, keepdims=True)
        scaled = dn * gain
        out = inv * scaled - x * (inv * inv * inv * jnp.mean(scaled * x, axis=1, keepdims=True))
        if j == 0:
            out = out + cots_ref[...].astype(F32)
        if fits:
            n_dev = ret_ref.shape[0]
            for lb in range(lane_blocks):
                piece = out[:, lb * LANES:(lb + 1) * LANES].reshape(n_dev, 8, LANES)
                ret_v[:, pl.ds((j * lane_blocks + lb) * 8, 8), :] = piece.astype(BF16)
            region = pl.ds(j * lane_blocks * 8, lane_blocks * 8)
            stores.append(pltpu.make_async_copy(ret_v.at[:, region], ret_ref.at[:, region], sems.at[4 + j]))
            stores[-1].start()
        else:
            ret_ref[j] = out.astype(BF16)
    if not fits:
        gain_out_ref[...] = gains
        att_out_ref[...] = att
        return
    base = slots * lane_blocks * 8
    feats = width // n_dev
    ret_v[:, pl.ds(base, feats), :] = att.reshape(n_dev, feats, LANES)
    high = gains.astype(BF16).astype(F32)
    low = gains - high
    row = iota((8, LANES), 0)
    for part, value in enumerate((high, low)):
        tile = jnp.zeros((8, LANES), F32)
        for lb in range(lane_blocks):
            tile = jnp.where(row == lb, value[:, lb * LANES:(lb + 1) * LANES], tile)
        tile = jnp.broadcast_to(tile.astype(BF16)[None], (n_dev, 8, LANES))
        ret_v[:, pl.ds(base + feats + part * 8, 8), :] = tile
    region = pl.ds(base, feats + 16)
    stores.append(pltpu.make_async_copy(ret_v.at[:, region], ret_ref.at[:, region], sems.at[4 + slots]))
    stores[-1].start()
    for store in stores:
        store.wait()


def finish_kernel(
    n_dev, slots, masks, norm_scale, place_ref, table_ref, back_ref, one_ref, *rest
):
    sources = rest[:len(masks)]
    out_ref, gw_ref, gain_ref, acc_ref, sems = rest[len(masks):len(masks) + 5]
    cots = rest[len(masks) + 5:]
    loads = [
        pltpu.make_async_copy(source, target, sems.at[at])
        for at, (source, target) in enumerate(zip(sources, cots))
    ]
    for load in loads:
        load.start()
    rows, width = out_ref.shape
    lane_blocks = width // LANES
    size = lane_blocks * 8
    acc_ref[...] = jnp.zeros_like(acc_ref)

    def add(dest, carry):
        for slot in range(slots):
            block = table_ref[dest, 0, rows + slot]
            acc_ref[block] += back_ref[dest, pl.ds(slot * size, size), :].astype(F32)
        return carry

    lax.fori_loop(0, n_dev, add, 0, unroll=2)
    upper, seat = place_ref[0], place_ref[1]
    me = upper * (n_dev // 2) + seat
    one = one_ref[upper]
    for lb in range(lane_blocks):
        total = acc_ref[:, pl.ds(lb * 8, 8), :].reshape(rows, LANES).astype(BF16)
        out_ref[:, pl.ds(lb * LANES, LANES)] = nn(one, total).astype(BF16)
    base = slots * size
    feats = width // n_dev
    acc = jnp.zeros((feats, width), F32)
    for group, ref, load in zip(masks, cots, loads):
        load.wait()
        att = jnp.concatenate([back_ref[me ^ mask, pl.ds(base, feats), :] for mask in group], axis=1)
        acc = acc + nn(att, ref[...])
    gw_ref[...] = acc * norm_scale
    tile = jnp.zeros((8, LANES), F32)
    for dest in range(n_dev):
        for part in range(2):
            tile = tile + back_ref[dest, pl.ds(base + feats + part * 8, 8), :].astype(F32)
    gain_ref[...] = tile * norm_scale


VM = pl.BlockSpec(memory_space=pltpu.VMEM)
SM = pl.BlockSpec(memory_space=pltpu.SMEM)
HB = pl.BlockSpec(memory_space=pltpu.HBM)


def near_core(x):
    return pltpu.with_memory_space_constraint(x, pltpu.VMEM)


def swap(block, mask):
    n_dev = lax.axis_size("ctx")
    return lax.ppermute(block, "ctx", [(i, i ^ mask) for i in range(n_dev)])


def per_device(
    raster_tokens, hilbert_perm, neighbors, neighbor_counts, norm_gain, w_qkv, w_out, cotangent
):
    n_dev = lax.axis_size("ctx")
    half = n_dev // 2
    me = lax.axis_index("ctx")
    rows, width = raster_tokens.shape
    slots = neighbors.shape[1]
    per_peer = rows // n_dev
    norm_scale = (rows * n_dev) ** (-0.5)
    n_rows = slots * BLOCK
    fits = per_peer % 8 == 0
    lane_blocks = width // LANES
    feats = width // n_dev
    place = jnp.stack([me // half, me % half]).astype(jnp.int32)
    note = pl.pallas_call(
        note_kernel,
        out_shape=jax.ShapeDtypeStruct((n_dev, 1, 2 * rows), jnp.int32),
        in_specs=[SM, VM],
        out_specs=VM,
    )(neighbors, hilbert_perm[None])
    mirror = swap(raster_tokens, half)
    other = swap(cotangent, half // 2)
    note = lax.all_to_all(note, "ctx", 0, 0, tiled=True)
    msg_shape = (half, 2, slots, per_peer, width) if fits else (8, LANES)
    sort_shape = (2, n_dev, per_peer, width) if fits else (2, rows, width)
    msg, one, *in_order = pl.pallas_call(
        functools.partial(pack_kernel, n_dev, slots, per_peer),
        out_shape=(
            jax.ShapeDtypeStruct(msg_shape, BF16),
            jax.ShapeDtypeStruct((2, rows, rows), BF16),
        ) + (() if fits else (jax.ShapeDtypeStruct(sort_shape, BF16),)),
        in_specs=[SM, SM] + [VM] * 3,
        out_specs=(VM,) * (2 if fits else 3),
        scratch_shapes=[pltpu.VMEM(sort_shape, BF16)] if fits else [],
    )(place, note, near_core(note), raster_tokens, near_core(mirror))
    table = note[:, 0, rows:rows + slots]
    if not fits:
        mine = lax.dynamic_slice_in_dim(table, place[0] * half, half, 0)
        msg = in_order[0].reshape(2, n_dev, per_peer, width)[:, mine].transpose(1, 0, 2, 3, 4)
    halves = [list(range(half)), list(range(half, n_dev))]
    arrived = lax.all_to_all(msg, "ctx", 0, 0, tiled=True, axis_index_groups=halves)
    held, cots, d_att, order = pl.pallas_call(
        ready_kernel,
        out_shape=(
            jax.ShapeDtypeStruct((2 * rows, width), BF16),
            jax.ShapeDtypeStruct((rows, width), BF16),
            jax.ShapeDtypeStruct((rows, width), BF16),
            jax.ShapeDtypeStruct((rows, rows), BF16),
        ),
        in_specs=[VM] * 4,
        out_specs=(VM,) * 4,
    )(cotangent, near_core(other), hilbert_perm[None], w_out)
    arrived, held = lax.optimization_barrier((arrived, held))
    names = [0, half // 2]
    bits = [1 << b for b in range(n_dev.bit_length() - 1)]
    for mask in [m for m in bits if m not in (1, 2, half, half // 2)]:
        held = jnp.concatenate([held, swap(held, mask)])
        names = names + [m ^ mask for m in names]
    across = swap(held, half)
    beside = swap(held, 2)
    if fits:
        ret_shape = (n_dev, slots * lane_blocks * 8 + feats + 16, LANES)
        extra_shapes = ()
    else:
        arrived = arrived.transpose(2, 1, 0, 3, 4).reshape(slots, rows, width)
        ret_shape = (slots, rows, width)
        extra_shapes = (
            jax.ShapeDtypeStruct((1, width), F32),
            jax.ShapeDtypeStruct((width, rows), BF16),
        )

    layer_out, ret, *extra = pl.pallas_call(
        functools.partial(main_kernel, fits),
        out_shape=(
            jax.ShapeDtypeStruct((rows, width), BF16),
            jax.ShapeDtypeStruct(ret_shape, BF16),
        ) + extra_shapes,
        in_specs=[SM] + [VM] * 5 + [HB] * 2,
        out_specs=(VM, HB if fits else VM) + (VM,) * len(extra_shapes),
        scratch_shapes=[
            pltpu.VMEM((n_rows, width), F32),
            pltpu.VMEM((n_rows, LANES), F32),
            pltpu.VMEM((n_rows, width), BF16),
            pltpu.VMEM((rows, width), BF16),
            pltpu.VMEM((n_rows, 2 * width), BF16),
            pltpu.VMEM((width, rows), BF16),
            pltpu.VMEM((rows, width), BF16),
            pltpu.VMEM((n_rows, 2 * width), BF16),
            pltpu.VMEM((n_rows, width), F32),
            pltpu.VMEM(w_qkv.shape, BF16),
            pltpu.VMEM(w_out.shape, BF16),
            pltpu.SemaphoreType.DMA((5 + slots,)),
            pltpu.VMEM(ret_shape if fits else (8, LANES), BF16),
        ],
        cost_estimate=pl.CostEstimate(
            flops=14 * n_rows * width * width, bytes_accessed=16 * width * width, transcendentals=0
        ),
    )(
        neighbor_counts, near_core(arrived), order, norm_gain[None], cots, d_att, w_qkv, w_out,
    )

    if fits:
        back = lax.all_to_all(ret, "ctx", 0, 0, tiled=True)
    corner = swap(across, 2)
    pieces = [
        (names, held),
        ([m ^ half for m in names], across),
        ([m ^ 2 for m in names], beside),
        ([m ^ 2 ^ half for m in names], corner),
    ]
    for group, piece in list(pieces):
        pieces.append(([m ^ 1 for m in group], swap(piece, 1)))
    if fits:
        masks = [group for group, piece in pieces]
        grad_tokens, grad_w_out, grad_gain = pl.pallas_call(
            functools.partial(finish_kernel, n_dev, slots, masks, norm_scale),
            out_shape=(
                jax.ShapeDtypeStruct((rows, width), BF16),
                jax.ShapeDtypeStruct((feats, width), F32),
                jax.ShapeDtypeStruct((lane_blocks, LANES), F32),
            ),
            in_specs=[SM, SM, VM, VM] + [HB] * len(pieces),
            out_specs=(VM, VM, VM),
            scratch_shapes=[
                pltpu.VMEM((n_dev, lane_blocks * 8, LANES), F32),
                pltpu.SemaphoreType.DMA((len(pieces),)),
            ] + [pltpu.VMEM(piece.shape, BF16) for group, piece in pieces],
        )(place, note, near_core(back), one, *[piece for group, piece in pieces])
        return (layer_out, grad_tokens, grad_w_out, grad_gain.reshape(width))
    gains, att = extra
    high = gains.astype(BF16)
    low = (gains - high.astype(F32)).astype(BF16)
    ret = ret.reshape(slots, n_dev, per_peer, width).transpose(1, 0, 2, 3).reshape(n_dev, -1)
    both = jnp.broadcast_to(jnp.concatenate([high, low]).reshape(1, -1), (n_dev, 2 * width))
    sizes = (ret.shape[1], feats * rows)
    ret = jnp.concatenate([ret, att.reshape(n_dev, -1), both], axis=1).reshape(n_dev, -1, LANES)
    back = lax.all_to_all(ret, "ctx", 0, 0, tiled=True).reshape(n_dev, -1)
    rest = back[:, :sizes[0]].reshape(n_dev * slots, per_peer, width).astype(F32)
    total = jnp.zeros((n_dev, per_peer, width), F32).at[table.reshape(-1)].add(rest)
    grad_tokens = nn(one[place[0]], total.reshape(rows, width).astype(BF16)).astype(BF16)
    att = back[:, sizes[0]:sizes[0] + sizes[1]].reshape(n_dev, feats, rows)
    order = me ^ jnp.array(sum([group for group, piece in pieces], []))
    cots = jnp.concatenate([piece for group, piece in pieces]).reshape(n_dev, rows, width)
    grad_w_out = jnp.einsum("sft,stw->fw", att[order], cots, preferred_element_type=F32) * norm_scale
    parts = back[:, sizes[0] + sizes[1]:].reshape(n_dev, 2, width).astype(F32)
    grad_gain = jnp.sum(parts, axis=(0, 1)) * norm_scale
    return (layer_out, grad_tokens, grad_w_out, grad_gain)


def solution(mesh):
    placed = (
        P(("groups", "ctx"), None),
        P(("groups", "ctx")),
        P(("groups", "ctx"), None),
        P(("groups", "ctx")),
        P(),
        P(),
        P(),
        P(("groups", "ctx"), None),
    )

    return jax.shard_map(
        per_device,
        mesh=mesh,
        in_specs=placed,
        out_specs=(
            P(("groups", "ctx"), None),
            P(("groups", "ctx"), None),
            P(("groups", "ctx"), None),
            P("groups"),
        ),
        check_vma=False,
    )
```
